32 devices in a mesh: shard: 16 (over z, y, x), replica: 2 (over core).
Axes of the slice: x: 2, y: 2, z: 4, core: 2. Of those that a mesh axis runs over, the one named last changes fastest.
Arguments:
- tokens: bfloat16 [32, 256, 768], P(('shard', 'replica')), may hold values from -6 to 6
- segment_ids: int32 [32, 256], P(('shard', 'replica')), may hold values from 0 to 7, never falling along the last dimension, each value on 1 to 128 neighbouring positions
- cotangent: bfloat16 [32, 256, 768], P(('shard', 'replica')), may hold values from -6 to 6
- w_qkv: float32 [768, 2304], P('shard'), may hold values from -5 to 5
- w_out: float32 [768, 768], P('shard'), may hold values from -0.625 to 0.625
- w_in: float32 [768, 3072], P('shard'), may hold values from -0.21875 to 0.21875
- w_down: float32 [3072, 768], P('shard'), may hold values from -0.109375 to 0.109375
- vectors: float32 [9984], P('shard'), may hold values from -1.5 to 1.5
- m_qkv: float32 [768, 2304], P('shard'), may hold values from -6 to 6
- m_out: float32 [768, 768], P('shard'), may hold values from -6 to 6
- m_in: float32 [768, 3072], P('shard'), may hold values from -6 to 6
- m_down: float32 [3072, 768], P('shard'), may hold values from -6 to 6
- m_vec: float32 [9984], P('shard'), may hold values from -6 to 6
- v_qkv: float32 [768, 2304], P('shard'), may hold values from 1 to 100
- v_out: float32 [768, 768], P('shard'), may hold values from 1 to 100
- v_in: float32 [768, 3072], P('shard'), may hold values from 1 to 100
- v_down: float32 [3072, 768], P('shard'), may hold values from 1 to 100
- v_vec: float32 [9984], P('shard'), may hold values from 1 to 100
Outputs:
- output: bfloat16 [32, 256, 768], P(('shard', 'replica'))
- input_grad: float32 [32, 256, 768], P(('shard', 'replica'))
- grad_qkv: float32 [768, 2304], P('shard')
- grad_out: float32 [768, 768], P('shard')
- grad_in: float32 [768, 3072], P('shard')
- grad_down: float32 [3072, 768], P('shard')
- grad_vec: float32 [9984], P('shard')
- new_qkv: float32 [768, 2304], P('shard')
- new_out: float32 [768, 768], P('shard')
- new_in: float32 [768, 3072], P('shard')
- new_down: float32 [3072, 768], P('shard')
- new_vec: float32 [9984], P('shard')
- new_m_qkv: float32 [768, 2304], P('shard')
- new_m_out: float32 [768, 768], P('shard')
- new_m_in: float32 [768, 3072], P('shard')
- new_m_down: float32 [3072, 768], P('shard')
- new_m_vec: float32 [9984], P('shard')
- new_v_qkv: float32 [768, 2304], P('shard')
- new_v_out: float32 [768, 768], P('shard')
- new_v_in: float32 [768, 3072], P('shard')
- new_v_down: float32 [3072, 768], P('shard')
- new_v_vec: float32 [9984], P('shard')
The draws below stay inside these ranges and needn't reach their ends.
Inputs may be any that keep to these rules, and one draw needn't show every extreme that they name: `segment_ids`: segment ids never fall along a sequence; each document has 1 to 128 tokens.
All inputs are finite; a program needn't handle non-finite values.
Results may differ from the reference program's by a relative error of at most 0.014.
Values may be sent and summed in bfloat16 or wider, within the bound.
No kernel may reach another device: no remote copies, remote signals or barrier semaphores. Data moves between devices by JAX's collectives and lax.ppermute only.
A program may use at most 128 MiB of HBM per device.

```python
import math
import jax
import jax.numpy as jnp
import numpy as np
from jax import lax

D = 768
HEADS = 12
HEAD_DIM = 64
FF = 3072
ROT = 16
SEQ_LEN = 256
DOCS = 8
STEP = 5
SEQS = 32
VEC = 9984


def draw_w_qkv(key, part):
    drawn = jnp.clip(jax.random.normal(key, (D, 3 * D), jnp.float32), -6.0, 6.0) * D ** (-0.5)
    return drawn


def draw_vectors(key, part):
    total = 9 * D + FF
    normal_part = jnp.clip(jax.random.normal(key, (total,), jnp.float32), -5.0, 5.0) * 0.3
    gain_part = jax.random.uniform(jax.random.fold_in(key, 3), (total,), jnp.float32, 0.5, 1.5)
    position = jnp.arange(total)
    is_gain = (position < D) | (position >= 2 * D) & (position < 3 * D)
    return jnp.where(is_gain, gain_part, normal_part)


def block_scale(own_key, shape, cuts, smallest, high):
    loudness = 1.0
    for dim, parts in cuts:
        steps = jax.random.uniform(jax.random.fold_in(jax.random.fold_in(own_key, 6), dim), (parts,), jnp.float32, smallest / len(cuts), high / len(cuts))
        loudness = loudness * jnp.repeat(jnp.exp(steps), shape[dim] // parts).reshape((-1,) + (1,) * (len(shape) - 1 - dim))
    return loudness


def profile(count, total, most, lean):
    loads = [(1 << 20) // math.isqrt(grade ** lean) + 1 for grade in range(2, count + 1)]
    surplus, holding = total - most - (count - 1), [1] * (count - 1)
    while surplus > 0:
        candidates = [i for i in range(count - 1) if holding[i] < most]
        pool, remaining = sum([loads[i] for i in candidates]), surplus
        for i in candidates:
            extra = min(most - holding[i], max(1, remaining * loads[i] // pool), surplus)
            holding[i] = holding[i] + extra
            surplus = surplus - extra
    return np.array([most] + holding)


def ragged(own_key, number_of, total, limit, slope):
    if number_of == 2:
        one = jax.random.randint(own_key, (), max(1, total - limit), min(limit, total - 1) + 1)
        return jnp.stack([one, total - one])
    sizes = jnp.asarray(profile(number_of, total, limit, slope), jnp.int32)
    pairs = (number_of - 1) // 2
    donor, sink = sizes[1:1 + 2 * pairs:2], sizes[2:2 + 2 * pairs:2]
    margin = jnp.minimum(donor - 1, limit - sink)
    passed = jax.random.randint(jax.random.fold_in(own_key, 1), (pairs,), 0, 1 << 20) % (margin + 1)
    sizes = sizes.at[1:1 + 2 * pairs:2].set(donor - passed).at[2:2 + 2 * pairs:2].set(sink + passed)
    return sizes[jax.random.permutation(jax.random.fold_in(own_key, 2), number_of)]


def gaussian(stream_key, shape, width, reach, pieces=(), held_as=jnp.bfloat16):
    array = jax.random.normal(stream_key, shape, jnp.float32) * width
    if len(pieces) > 0:
        array = block_scale(stream_key, shape, pieces, -0.22, 0.18) * array
    return jnp.clip(array, min=-reach, max=reach).astype(held_as)


def setup_inputs(seed: int = 0) -> dict:
    key_list = jax.random.split(jax.random.key(seed), 19)
    return {
        "tokens": gaussian(key_list[0], (SEQS, SEQ_LEN, D), 1.0, 6.0, ((0, 32),)),
        "segment_ids": jax.vmap(lambda own: jnp.searchsorted(jnp.cumsum(ragged(own, DOCS, SEQ_LEN, SEQ_LEN // 2, 1)), jnp.arange(SEQ_LEN), side="right"))(jax.random.split(key_list[1], SEQS)).reshape((SEQS, SEQ_LEN)).astype(jnp.int32),
        "cotangent": gaussian(key_list[2], (SEQS, SEQ_LEN, D), 1.0, 6.0, ((0, 32),)),
        "w_qkv": draw_w_qkv(jax.random.fold_in(key_list[18], 71), 0),
        "w_out": gaussian(key_list[4], (D, D), (D // 8) ** -0.5, 0.625, ((0, 16),), jnp.float32),
        "w_in": gaussian(key_list[5], (D, FF), D ** -0.5, 0.21875, ((0, 16),), jnp.float32),
        "w_down": gaussian(key_list[6], (FF, D), FF ** -0.5, 0.109375, ((0, 16),), jnp.float32),
        "vectors": draw_vectors(jax.random.fold_in(key_list[18], 71), 0),
        "m_qkv": gaussian(key_list[8], (D, 3 * D), 1.0, 6.0, ((0, 16),), jnp.float32),
        "m_out": gaussian(key_list[9], (D, D), 1.0, 6.0, ((0, 16),), jnp.float32),
        "m_in": gaussian(key_list[10], (D, FF), 1.0, 6.0, ((0, 16),), jnp.float32),
        "m_down": gaussian(key_list[11], (FF, D), 1.0, 6.0, ((0, 16),), jnp.float32),
        "m_vec": gaussian(key_list[12], (VEC,), 1.0, 6.0, ((0, 16),), jnp.float32),
        "v_qkv": jnp.clip(jnp.exp(math.log(100.0) - 4.6051702 * jax.random.uniform(key_list[13], (D, 3 * D), jnp.float32) ** block_scale(key_list[13], (D, 3 * D), ((0, 16),), -0.2, 0.2)), 1.0, 100.0),
        "v_out": jnp.clip(jnp.exp(math.log(100.0) - 4.6051702 * jax.random.uniform(key_list[14], (D, D), jnp.float32) ** block_scale(key_list[14], (D, D), ((0, 16),), -0.2, 0.2)), 1.0, 100.0),
        "v_in": jnp.clip(jnp.exp(math.log(100.0) - 4.6051702 * jax.random.uniform(key_list[15], (D, FF), jnp.float32) ** block_scale(key_list[15], (D, FF), ((0, 16),), -0.2, 0.2)), 1.0, 100.0),
        "v_down": jnp.clip(jnp.exp(math.log(100.0) - 4.6051702 * jax.random.uniform(key_list[16], (FF, D), jnp.float32) ** block_scale(key_list[16], (FF, D), ((0, 16),), -0.2, 0.2)), 1.0, 100.0),
        "v_vec": jnp.clip(jnp.exp(math.log(100.0) - 4.6051702 * jax.random.uniform(key_list[17], (VEC,), jnp.float32) ** block_scale(key_list[17], (VEC,), ((0, 16),), -0.2, 0.2)), 1.0, 100.0),
    }


norm_eps = 1e-05
learn_rate = 0.01
beta_first = 0.9
beta_second = 0.999
adam_eps = 1e-08
decay_rate = 0.1

def layer_norm(values, gain_vec, offset):
    center = values - lax.optimization_barrier(jnp.mean(values, axis=-1, keepdims=True))
    spread = lax.optimization_barrier(jnp.mean(center * center, axis=-1, keepdims=True))
    return center * lax.rsqrt(spread + norm_eps) * gain_vec + offset

def gelu_exact(values):
    return jax.nn.gelu(values, approximate=False)

def rotary_tables(length):
    half_rot = ROT // 2
    freqs = 10000.0 ** (-jnp.arange(half_rot, dtype=jnp.float32) * 2.0 / ROT)
    angles = jnp.arange(length, dtype=jnp.float32)[:, None] * freqs[None, :]
    return (jnp.cos(angles), jnp.sin(angles))

def rotate(values, cosine, sine_table):
    half_rot = ROT // 2
    lower_part = values[..., :half_rot]
    upper_part = values[..., half_rot:ROT]
    return jnp.concatenate([lower_part * cosine - upper_part * sine_table, upper_part * cosine + lower_part * sine_table, values[..., ROT:]], axis=-1)

def split_vectors(vectors):
    bounds = [0, D, 2 * D, 3 * D, 4 * D, 7 * D, 8 * D, 8 * D + FF, 9 * D + FF]
    return [vectors[bounds[number]:bounds[number + 1]] for number in range(8)]

def attention_mask(segment_ids):
    length = segment_ids.shape[1]
    same_doc = segment_ids[:, :, None] == segment_ids[:, None, :]
    causal = jnp.arange(length)[:, None] >= jnp.arange(length)[None, :]
    return (same_doc & causal[None])[:, None]

def attention_scores(query, keyed, allowed):
    raw_scores = jnp.einsum('shqd,shkd->shqk', query.astype(jnp.float32), keyed.astype(jnp.float32)) * HEAD_DIM ** (-0.5)
    return jnp.where(allowed, raw_scores, -1e+30)

def forward(tokens, segment_ids, params):
    w_qkv, w_out, w_in, w_down, vectors = params
    gain_one, offset_one, gain_two, offset_two, bias_qkv, bias_out, bias_in, bias_down = split_vectors(vectors.astype(jnp.float32))
    seq_count = tokens.shape[0]
    length = tokens.shape[1]
    inputs = tokens.reshape(seq_count * length, D).astype(jnp.float32)
    normed_attn = layer_norm(inputs, gain_one, offset_one).astype(jnp.bfloat16)
    normed_mlp = layer_norm(inputs, gain_two, offset_two).astype(jnp.bfloat16)
    projected = jnp.dot(normed_attn, w_qkv, preferred_element_type=jnp.float32) + bias_qkv
    heads_view = projected.reshape(seq_count, length, 3, HEADS, HEAD_DIM).transpose(2, 0, 3, 1, 4)
    cosine, sine_table = rotary_tables(length)
    query = rotate(heads_view[0], cosine, sine_table).astype(jnp.bfloat16)
    keyed = rotate(heads_view[1], cosine, sine_table).astype(jnp.bfloat16)
    valued = heads_view[2].astype(jnp.bfloat16)
    allowed = attention_mask(segment_ids)
    scores = attention_scores(query, keyed, allowed)
    top_score = lax.optimization_barrier(jnp.max(scores, axis=-1, keepdims=True))
    log_total = top_score + jnp.log(lax.optimization_barrier(jnp.sum(jnp.exp(scores - top_score), axis=-1, keepdims=True)))
    attn_probs = jnp.where(allowed, jnp.exp(scores - log_total), 0.0).astype(jnp.bfloat16)
    mixed = jnp.einsum('shqk,shkd->shqd', attn_probs.astype(jnp.float32), valued.astype(jnp.float32))
    mixed = mixed.transpose(0, 2, 1, 3).reshape(seq_count * length, D).astype(jnp.bfloat16)
    attn_branch = jnp.dot(mixed, w_out, preferred_element_type=jnp.float32) + bias_out
    hidden = jnp.dot(normed_mlp, w_in, preferred_element_type=jnp.float32) + bias_in
    act_half = gelu_exact(hidden).astype(jnp.bfloat16)
    mlp_branch = jnp.dot(act_half, w_down, preferred_element_type=jnp.float32) + bias_down
    output = (inputs + attn_branch + mlp_branch).astype(jnp.bfloat16).reshape(seq_count, length, D)
    saved = (inputs, normed_attn, normed_mlp, query, keyed, valued, allowed, log_total, mixed, hidden, act_half)
    return (output, saved)

def backward(cotangent, params, saved):
    w_qkv, w_out, w_in, w_down, vectors = params
    gain_one, offset_one, gain_two, offset_two, bias_qkv, bias_out, bias_in, bias_down = split_vectors(vectors.astype(jnp.float32))
    inputs, normed_attn, normed_mlp, query, keyed, valued, allowed, log_total, mixed, hidden, act_half = saved
    seq_count = query.shape[0]
    length = query.shape[2]
    grad_half = cotangent.reshape(seq_count * length, D)
    grad_full = grad_half.astype(jnp.float32)
    grad_down = jnp.dot(act_half.T, grad_half, preferred_element_type=jnp.float32)
    grad_act = jnp.dot(grad_half, w_down.T, preferred_element_type=jnp.float32)
    grad_hidden = jax.vjp(gelu_exact, hidden)[1](grad_act)[0]
    hidden_half = grad_hidden.astype(jnp.bfloat16)
    grad_in = jnp.dot(normed_mlp.T, hidden_half, preferred_element_type=jnp.float32)
    grad_normed_mlp = jnp.dot(hidden_half, w_in.T, preferred_element_type=jnp.float32)
    grad_out = jnp.dot(mixed.T, grad_half, preferred_element_type=jnp.float32)
    grad_mixed = jnp.dot(grad_half, w_out.T, preferred_element_type=jnp.float32).astype(jnp.bfloat16)
    grad_mixed = grad_mixed.reshape(seq_count, length, HEADS, HEAD_DIM).transpose(0, 2, 1, 3).astype(jnp.float32)
    scores = attention_scores(query, keyed, allowed)
    probs_full = jnp.where(allowed, jnp.exp(scores - log_total), 0.0)
    attn_probs = probs_full.astype(jnp.bfloat16).astype(jnp.float32)
    grad_value = jnp.einsum('shqk,shqd->shkd', attn_probs, grad_mixed)
    grad_probs = jnp.einsum('shqd,shkd->shqk', grad_mixed, valued.astype(jnp.float32))
    inner = lax.optimization_barrier(jnp.sum(probs_full * grad_probs, axis=-1, keepdims=True))
    grad_scores = (probs_full * (grad_probs - inner) * HEAD_DIM ** (-0.5)).astype(jnp.bfloat16).astype(jnp.float32)
    grad_query = jnp.einsum('shqk,shkd->shqd', grad_scores, keyed.astype(jnp.float32))
    grad_key = jnp.einsum('shqk,shqd->shkd', grad_scores, query.astype(jnp.float32))
    cosine, sine_table = rotary_tables(length)
    grad_query = rotate(grad_query, cosine, -sine_table)
    grad_key = rotate(grad_key, cosine, -sine_table)
    grad_projected = jnp.stack([grad_query, grad_key, grad_value]).transpose(1, 3, 0, 2, 4).reshape(seq_count * length, 3 * D)
    projected_half = grad_projected.astype(jnp.bfloat16)
    grad_qkv = jnp.dot(normed_attn.T, projected_half, preferred_element_type=jnp.float32)
    grad_normed_attn = jnp.dot(projected_half, w_qkv.T, preferred_element_type=jnp.float32)
    norm_one_vjp = jax.vjp(layer_norm, inputs, gain_one, offset_one)[1]
    back_one, grad_gain_one, grad_offset_one = norm_one_vjp(grad_normed_attn)
    norm_two_vjp = jax.vjp(layer_norm, inputs, gain_two, offset_two)[1]
    back_two, grad_gain_two, grad_offset_two = norm_two_vjp(grad_normed_mlp)
    input_grad = (grad_full + back_one + back_two).reshape(seq_count, length, D)
    column_sum = lax.optimization_barrier(jnp.sum(grad_full, axis=0))
    vector_grad = jnp.concatenate([grad_gain_one, grad_offset_one, grad_gain_two, grad_offset_two, lax.optimization_barrier(jnp.sum(grad_projected, axis=0)), column_sum, lax.optimization_barrier(jnp.sum(grad_hidden, axis=0)), column_sum])
    return (input_grad, (grad_qkv, grad_out, grad_in, grad_down, vector_grad))

def adamw(weight, gradient, moment_one, moment_two, decay_on):
    moment_one = beta_first * moment_one + (1.0 - beta_first) * gradient
    moment_two = beta_second * moment_two + (1.0 - beta_second) * gradient * gradient
    first_hat = moment_one / (1.0 - beta_first ** STEP)
    second_hat = moment_two / (1.0 - beta_second ** STEP)
    updated = weight - learn_rate * (first_hat / (jnp.sqrt(second_hat) + adam_eps) + decay_on * weight)
    return (updated, moment_one, moment_two)

def reference(tokens, segment_ids, cotangent, w_qkv, w_out, w_in, w_down, vectors, m_qkv, m_out, m_in, m_down, m_vec, v_qkv, v_out, v_in, v_down, v_vec):
    masters = (w_qkv, w_out, w_in, w_down, vectors)
    params = tuple((weight.astype(jnp.bfloat16) for weight in masters))
    block_size = 16
    n_blocks = SEQS // block_size

    def block_step(totals, inputs):
        block_tokens, block_segments, block_cot = inputs
        output, saved = forward(block_tokens, block_segments, params)
        input_grad, gradients = backward(block_cot, params, saved)
        totals = tuple((total + gradient for total, gradient in zip(totals, gradients)))
        return (totals, (output, input_grad))
    initial = tuple((jnp.zeros(weight.shape, jnp.float32) for weight in masters))
    scanned = (tokens.reshape(n_blocks, block_size, SEQ_LEN, D), segment_ids.reshape(n_blocks, block_size, SEQ_LEN), cotangent.reshape(n_blocks, block_size, SEQ_LEN, D))
    totals, (outputs, input_grads) = lax.scan(block_step, initial, scanned)
    output = outputs.reshape(SEQS, SEQ_LEN, D)
    input_grad = input_grads.reshape(SEQS, SEQ_LEN, D)
    firsts = (m_qkv, m_out, m_in, m_down, m_vec)
    seconds = (v_qkv, v_out, v_in, v_down, v_vec)
    decays = (decay_rate, decay_rate, decay_rate, decay_rate, 0.0)
    results = [adamw(masters[number], totals[number], firsts[number], seconds[number], decays[number]) for number in range(5)]
    return (output, input_grad, totals[0], totals[1], totals[2], totals[3], totals[4], results[0][0], results[1][0], results[2][0], results[3][0], results[4][0], results[0][1], results[1][1], results[2][1], results[3][1], results[4][1], results[0][2], results[1][2], results[2][2], results[3][2], results[4][2])
```

```python
import functools

import jax
import jax.numpy as jnp
import numpy as np
from jax import lax
from jax.experimental import pallas as pl
from jax.experimental.pallas import tpu as pltpu
from jax.sharding import PartitionSpec as P

D = 768
HEADS = 12
HEAD_DIM = 64
FF = 3072
ROT = 16
STEP = 5


norm_eps = 1e-05
learn_rate = 0.01
beta_first = 0.9
beta_second = 0.999
adam_eps = 1e-08
decay_rate = 0.1


def split_vectors(vectors):
    bounds = [0, D, 2 * D, 3 * D, 4 * D, 7 * D, 8 * D, 8 * D + FF, 9 * D + FF]
    return [vectors[bounds[number] : bounds[number + 1]] for number in range(8)]


def rotary_lanes(length, heads):
    half_rot = ROT // 2
    freqs = 10000.0 ** (-np.arange(half_rot) * 2.0 / ROT)
    angles = np.arange(length)[:, None] * freqs[None, :]
    cosine = np.ones((length, HEAD_DIM))
    sine = np.zeros((length, HEAD_DIM))
    cosine[:, :ROT] = np.tile(np.cos(angles), (1, 2))
    sine[:, :ROT] = np.tile(np.sin(angles), (1, 2))
    partner = np.zeros((HEAD_DIM, HEAD_DIM))
    for lane in range(half_rot):
        partner[lane + half_rot, lane] = -1.0
        partner[lane, lane + half_rot] = 1.0
    cosine = jnp.tile(jnp.asarray(cosine, jnp.float32), (1, heads))
    sine = jnp.tile(jnp.asarray(sine, jnp.float32), (1, heads))
    return cosine, sine, jnp.asarray(np.kron(np.eye(heads), partner), jnp.bfloat16)


def contract(left, right, left_dim, right_dim):
    return lax.dot_general(
        left, right, (((left_dim,), (right_dim,)), ((), ())), preferred_element_type=jnp.float32
    )


def attention_kernel(
    ways,
    heads,
    normed_ref,
    cot_ref,
    seg_col_ref,
    seg_row_ref,
    qkv_ref,
    out_ref,
    bias_ref,
    cos_ref,
    sin_ref,
    partner_ref,
    mixed_ref,
    branch_ref,
    slope_ref,
    sums_ref,
    grad_qkv_ref,
    grad_out_ref,
    qkv_total,
    out_total,
):
    half = jnp.bfloat16
    wide = jnp.float32
    step = pl.program_id(0)
    cols = heads * HEAD_DIM
    cosine, sine, partner = cos_ref[...], sin_ref[...], partner_ref[...]

    def partners(values):
        high = values.astype(half)
        low = (values - high.astype(wide)).astype(half)
        return contract(high, partner, 1, 0) + contract(low, partner, 1, 0)

    normed = normed_ref[...]
    cot = cot_ref[...]
    projected = contract(normed, qkv_ref[...], 1, 0) + bias_ref[...]
    query, keyed = projected[:, :cols], projected[:, cols : 2 * cols]
    query = (query * cosine + partners(query) * sine).astype(half)
    keyed = (keyed * cosine + partners(keyed) * sine).astype(half)
    valued = projected[:, 2 * cols : 3 * cols].astype(half)
    grad_mixed = contract(cot, out_ref[...], 1, 1).astype(half)
    length = normed.shape[0]
    row = lax.broadcasted_iota(jnp.int32, (length, length), 0)
    column = lax.broadcasted_iota(jnp.int32, (length, length), 1)
    allowed = (seg_col_ref[0] == seg_row_ref[0]) & (row >= column)
    mixed, grad_q, grad_k, grad_v = [], [], [], []
    for head in range(heads):
        lanes = slice(head * HEAD_DIM, (head + 1) * HEAD_DIM)
        q, k, v, g = query[:, lanes], keyed[:, lanes], valued[:, lanes], grad_mixed[:, lanes]
        scores = jnp.where(allowed, contract(q, k, 1, 1) * HEAD_DIM ** (-0.5), -1e30)
        shifted = jnp.exp(scores - jnp.max(scores, axis=1, keepdims=True))
        probs_full = shifted / jnp.sum(shifted, axis=1, keepdims=True)
        probs = probs_full.astype(half)
        mixed.append(contract(probs, v, 1, 0))
        grad_v.append(contract(probs, g, 0, 0))
        grad_probs = contract(g, v, 1, 1)
        inner = jnp.sum(probs_full * grad_probs, axis=1, keepdims=True)
        grad_scores = (probs_full * (grad_probs - inner) * HEAD_DIM ** (-0.5)).astype(half)
        grad_q.append(contract(grad_scores, k, 1, 0))
        grad_k.append(contract(grad_scores, q, 0, 0))
    mixed = jnp.concatenate(mixed, axis=1).astype(half)
    grad_q = jnp.concatenate(grad_q, axis=1)
    grad_k = jnp.concatenate(grad_k, axis=1)
    grad_v = jnp.concatenate(grad_v, axis=1)
    grad_q = grad_q * cosine - partners(grad_q) * sine
    grad_k = grad_k * cosine - partners(grad_k) * sine
    grad_projected = jnp.concatenate([grad_q, grad_k, grad_v, jnp.zeros_like(grad_v)], axis=1)
    projected_half = grad_projected.astype(half)
    sums_ref[0] = jnp.sum(grad_projected, axis=0, keepdims=True)
    mixed_ref[...] = mixed
    branch_ref[...] = contract(mixed, out_ref[...], 1, 0)
    slope_ref[...] = contract(projected_half, qkv_ref[...], 1, 1)

    @pl.when(step == 0)
    def _():
        qkv_total[...] = jnp.zeros_like(qkv_total)
        out_total[...] = jnp.zeros_like(out_total)

    qkv_total[...] += contract(normed, projected_half, 0, 0)
    out_total[...] += contract(mixed, cot, 0, 0)

    @pl.when(step == pl.num_programs(0) - 1)
    def _():
        grad_qkv_ref[...] = qkv_total[...].astype(half)
        for way in range(ways):
            grad_out_ref[way] = out_total[:, way * cols : (way + 1) * cols].astype(half)


def attention(normed, cot, seg, qkv_all, out_all, bias, ways, heads):
    half = jnp.bfloat16
    wide = jnp.float32
    seqs, length = seg.shape
    count = seqs * length
    cols = heads * HEAD_DIM
    width = qkv_all.shape[1]
    cosine, sine, partner = rotary_lanes(length, heads)
    bias_row = jnp.pad(bias, (0, width - 3 * cols))[None]

    def block(rows, lanes):
        return pl.BlockSpec((rows, lanes), lambda s: (s, 0))

    def whole(*shape):
        return pl.BlockSpec(shape, lambda s: (0,) * len(shape))

    flops = 2 * count * (2 * D * width * 2 + 3 * D * cols + 7 * length * cols)
    return pl.pallas_call(
        functools.partial(attention_kernel, ways, heads),
        grid=(seqs,),
        in_specs=[
            block(length, D),
            block(length, D),
            pl.BlockSpec((1, length, 1), lambda s: (s, 0, 0)),
            pl.BlockSpec((1, 1, length), lambda s: (s, 0, 0)),
            whole(D, width),
            whole(cols, D),
            whole(1, width),
            whole(length, cols),
            whole(length, cols),
            whole(cols, cols),
        ],
        out_specs=[
            block(length, cols),
            block(length, D),
            block(length, D),
            pl.BlockSpec((1, 1, width), lambda s: (s, 0, 0)),
            whole(D, width),
            whole(ways, cols, cols),
        ],
        out_shape=[
            jax.ShapeDtypeStruct((count, cols), half),
            jax.ShapeDtypeStruct((count, D), wide),
            jax.ShapeDtypeStruct((count, D), wide),
            jax.ShapeDtypeStruct((seqs, 1, width), wide),
            jax.ShapeDtypeStruct((D, width), half),
            jax.ShapeDtypeStruct((ways, cols, cols), half),
        ],
        scratch_shapes=[pltpu.VMEM((D, width), wide), pltpu.VMEM((cols, D), wide)],
        compiler_params=pltpu.CompilerParams(dimension_semantics=("arbitrary",)),
        cost_estimate=pl.CostEstimate(
            flops=flops, bytes_accessed=18 * 1024 * 1024, transcendentals=seqs * heads * length**2
        ),
        name="attention_block",
    )(
        normed,
        cot,
        seg[:, :, None],
        seg[:, None, :],
        qkv_all,
        out_all,
        bias_row,
        cosine,
        sine,
        partner,
    )


class Group:
    def __init__(self, mesh):
        self.shards = mesh.shape["shard"]
        self.replicas = mesh.shape["replica"]
        self.rings = self.shards <= 16 and self.shards % 4 == 0
        self.twins = 2 if self.rings and HEADS % (2 * self.replicas) == 0 else 1
        self.ways = self.twins * self.replicas
        self.groups = self.shards // self.twins
        self.pairs = 2 if self.groups % 2 == 0 else 1
        self.lines = self.groups // self.pairs

    def place(self):
        shard = lax.axis_index("shard")
        self.shard = shard
        self.twin = shard % self.twins
        self.group = shard // self.twins
        self.pair = self.group % self.pairs
        self.line = self.group // self.pairs
        self.replica = lax.axis_index("replica")
        self.rank = self.twin * self.replicas + self.replica


    def from_twin(self, array):
        return lax.ppermute(array, "shard", [(s, s ^ 1) for s in range(self.shards)])

    def from_pair(self, array):
        step = self.twins
        return lax.ppermute(array, "shard", [(s, s ^ step) for s in range(self.shards)])

    def along_line(self, array, hops):
        block = self.twins * self.pairs
        return lax.ppermute(
            array,
            "shard",
            [
                (s, ((s // block + hops) % self.lines) * block + s % block)
                for s in range(self.shards)
            ],
        )

    def to_replica(self, array, hops):
        size = self.replicas
        return lax.ppermute(array, "replica", [(c, (c + hops) % size) for c in range(size)])

    def twins_in_order(self, own, far):
        return jnp.stack(
            [jnp.where(self.twin == 0, own, far), jnp.where(self.twin == 0, far, own)]
        )

    def to_rank(self, array, twin_flip, hops):
        size = self.replicas
        pairs = [
            (s * size + c, (s ^ twin_flip) * size + (c + hops) % size)
            for s in range(self.shards)
            for c in range(size)
        ]
        return lax.ppermute(array, ("shard", "replica"), pairs)


    def gather(self, piece, after=None, direct=False):
        if not self.rings:
            return lax.all_gather(piece, "shard", axis=0, tiled=False), None
        if after is not None:
            piece, _ = lax.optimization_barrier((piece, after))
        held = [piece]
        for hops in range(1, self.lines):
            if direct:
                held.append(self.along_line(piece, hops))
            else:
                held.append(self.along_line(held[-1], 1))
        buffer = jnp.zeros((self.groups,) + piece.shape, piece.dtype)
        zeros = (0,) * piece.ndim
        for hops, block in enumerate(held):
            line = (self.line - hops) % self.lines
            own = line * self.pairs + self.pair
            buffer = lax.dynamic_update_slice(buffer, block[None], (own,) + zeros)
        for hops, block in enumerate(held):
            line = (self.line - hops) % self.lines
            other = line * self.pairs + (self.pair ^ 1)
            buffer = lax.dynamic_update_slice(
                buffer, self.from_pair(block)[None], (other,) + zeros
            )
        return buffer, held[-1]

    def scatter(self, terms, pieces=1):
        wide = jnp.float32
        if not self.rings:
            total = lax.psum_scatter(terms.astype(wide), "shard", scatter_dimension=0, tiled=False)
            return total
        halves = terms.reshape((self.lines, self.pairs) + terms.shape[1:])
        keep = lax.dynamic_index_in_dim(halves, self.pair, 1, keepdims=False)
        give = lax.dynamic_index_in_dim(halves, self.pair ^ 1, 1, keepdims=False)

        def block(array, hops):
            return lax.dynamic_index_in_dim(
                array, (self.line + hops) % self.lines, 0, keepdims=False
            )

        order = [hops for hops in range(1, self.lines)] + [0]
        if pieces == 1:
            merged = keep.astype(wide) + self.from_pair(give).astype(wide)
            sums = {hops: block(merged, hops) for hops in order}
        else:
            sums = {}
            size = -(-self.lines // pieces)
            for start in range(0, self.lines, size):
                chosen = order[start : start + size]
                far = self.from_pair(jnp.stack([block(give, hops) for hops in chosen]))
                for place, hops in enumerate(chosen):
                    sums[hops] = block(keep, hops).astype(wide) + far[place].astype(wide)
        total = sums[0]
        for hops in range(1, self.lines):
            total = total + self.along_line(sums[hops].astype(jnp.bfloat16), hops).astype(wide)
        return total

    def gather_sequences(self, array):
        across = array[None]
        if self.twins == 2:
            across = jnp.stack([array, self.from_twin(array)])
        slots = [across]
        for hops in range(1, self.replicas):
            slots.append(self.to_replica(across, self.replicas - hops))
        return jnp.stack(slots).reshape((-1,) + array.shape[1:])

    def reduce_sequences(self, partial):
        wire = jnp.bfloat16
        wide = jnp.float32
        shape = partial.shape
        batch = shape[0] // self.ways
        slots = partial.reshape((self.replicas, self.twins, batch) + shape[1:])
        total = slots[0]
        for hops in range(1, self.replicas):
            total = total + self.to_replica(slots[hops].astype(wire), hops).astype(wide)
        own = total[0]
        if self.twins == 2:
            own = own + self.from_twin(total[1].astype(wire)).astype(wide)
        return own


    def share(self, pick):
        own = pick(self.rank)
        if self.twins == 1:
            return own[None]
        far = self.from_twin(pick((self.twin ^ 1) * self.replicas + self.replica))
        return self.twins_in_order(own, far)

    def from_replicas(self, own):
        held = [own] + [self.to_replica(own, hops) for hops in range(1, self.replicas)]
        if self.replicas == 2:
            return jnp.stack(
                [
                    jnp.where(self.replica == 0, held[0], held[1]),
                    jnp.where(self.replica == 0, held[1], held[0]),
                ]
            )
        result = jnp.zeros((self.replicas,) + own.shape, own.dtype)
        for hops, part in enumerate(held):
            source = (self.replica - hops) % self.replicas
            result = lax.dynamic_update_slice(result, part[None], (source,) + (0,) * own.ndim)
        return result

    def unshare(self, rows):
        half = jnp.bfloat16
        own = lax.dynamic_index_in_dim(rows, self.twin, 0, keepdims=False).astype(half)
        if self.twins == 2:
            give = lax.dynamic_index_in_dim(rows, self.twin ^ 1, 0, keepdims=False)
            both = self.twins_in_order(own, self.from_twin(give.astype(half)))
        else:
            both = own[None]
        stacked = jnp.swapaxes(self.from_replicas(both), 0, 1)
        return stacked.reshape((self.ways,) + own.shape)

    def exchange(self, blocks):
        held = {}
        for flip in range(self.twins):
            for hops in range(self.replicas):
                target = (self.twin ^ flip) * self.replicas + (
                    self.replica + hops
                ) % self.replicas
                block = lax.dynamic_index_in_dim(blocks, target, 0, keepdims=False)
                if flip or hops:
                    block = self.to_rank(block, flip, hops)
                held[flip, hops] = block

        def source(rank):
            twin, replica = rank // self.replicas, rank % self.replicas
            flip = self.twin ^ twin
            hops = (self.replica - replica) % self.replicas
            block = held[0, 0]
            for key in list(held)[1:]:
                block = jnp.where((flip == key[0]) & (hops == key[1]), held[key], block)
            return block

        return [source(rank) for rank in range(self.ways)]


def adamw(weight, gradient, moment_one, moment_two, decay_on):
    moment_one = beta_first * moment_one + (1.0 - beta_first) * gradient
    moment_two = beta_second * moment_two + (1.0 - beta_second) * gradient * gradient
    first_hat = moment_one / (1.0 - beta_first**STEP)
    second_hat = moment_two / (1.0 - beta_second**STEP)
    updated = weight - learn_rate * (
        first_hat / (jnp.sqrt(second_hat) + adam_eps) + decay_on * weight
    )
    return (updated, moment_one, moment_two)

def body(
    group,
    tokens,
    segment_ids,
    cotangent,
    w_qkv,
    w_out,
    w_in,
    w_down,
    vectors,
    m_qkv,
    m_out,
    m_in,
    m_down,
    m_vec,
    v_qkv,
    v_out,
    v_in,
    v_down,
    v_vec,
):
    group.place()
    half = jnp.bfloat16
    wide = jnp.float32
    ways = group.ways
    groups = group.groups
    twins = group.twins
    heads = HEADS // ways
    rows = w_qkv.shape[0]
    units = FF // (groups * ways)
    out_cols = D // ways
    width = 4 * out_cols
    batch, length = tokens.shape[:2]
    seqs = batch * ways
    count = seqs * length
    vec_size = vectors.shape[0]
    vec_rows = -(-vec_size // (8 * width)) * 8

    seg_rows = jnp.pad(segment_ids.astype(half)[:, None], ((0, 0), (0, 7), (0, D - length)))
    pack = jnp.concatenate([tokens, cotangent, seg_rows], axis=1)
    packs = group.gather_sequences(pack)
    x_seqs = packs[:, :length]
    cot = packs[:, length : 2 * length]
    seg = packs[:, 2 * length, :length].astype(wide)

    qkv_half = w_qkv.astype(half).reshape(rows, 3, ways, out_cols)
    out_half = w_out.astype(half).reshape(rows, ways, out_cols)
    in_half = w_in.astype(half).reshape(rows, groups, ways, units)
    down_half = w_down.astype(half).reshape(group.replicas, units, D)
    vec_half = jnp.pad(vectors.astype(half), (0, vec_rows * width - vec_size))
    vec_half = vec_half.reshape(vec_rows, width)

    def pick_first(rank):
        qkv = lax.dynamic_index_in_dim(qkv_half, rank, 2, keepdims=False).reshape(rows, -1)
        out = lax.dynamic_index_in_dim(out_half, rank, 1, keepdims=False)
        return jnp.concatenate([jnp.concatenate([qkv, out], axis=1), vec_half], axis=0)

    def pick_in(rank):
        return lax.dynamic_index_in_dim(in_half, rank, 2, keepdims=False).reshape(rows, -1)

    down_piece = lax.dynamic_index_in_dim(down_half, group.replica, 0, keepdims=False)
    first, done = group.gather(group.share(pick_first), direct=True)
    second_piece = jnp.concatenate(
        [group.share(pick_in).reshape(-1, width), down_piece.reshape(-1, width)], axis=0
    )
    second, _ = group.gather(second_piece, done)
    qkv_all = first[:, :, :rows].reshape(D, width)
    vec_all = first[:, :, rows:].reshape(group.shards, -1)[:, :vec_size].reshape(-1).astype(wide)
    in_all = second[:, : twins * rows].reshape(D, width)
    down_all = second[:, twins * rows :].reshape(width, D)
    out_all = group.exchange(qkv_all[:, 3 * out_cols :].reshape(ways, out_cols, out_cols))
    out_all = jnp.concatenate(out_all, axis=1)

    gain_one, offset_one, gain_two, offset_two, bias_qkv, bias_out, bias_in, bias_down = (
        split_vectors(vec_all)
    )
    bias_qkv_own = lax.dynamic_index_in_dim(
        bias_qkv.reshape(3, ways, -1), group.rank, 1, keepdims=False
    ).reshape(-1)
    bias_in_own = lax.dynamic_index_in_dim(
        bias_in.reshape(groups, ways, units), group.rank, 1, keepdims=False
    ).reshape(-1)

    inputs = x_seqs.reshape(count, D).astype(wide)
    center = inputs - jnp.mean(inputs, axis=-1, keepdims=True)
    spread = jnp.mean(center * center, axis=-1, keepdims=True)
    unit = center * lax.rsqrt(spread + norm_eps)
    normed_attn = (unit * gain_one + offset_one).astype(half)
    normed_mlp = (unit * gain_two + offset_two).astype(half)
    cot_flat = cot.reshape(count, D)
    mixed, branch_attn, partial_attn, sums_attn, grad_qkv, grad_out = attention(
        normed_attn, cot_flat, seg, qkv_all, out_all, bias_qkv_own, ways, heads
    )
    bias_qkv_grad = jnp.sum(sums_attn, axis=(0, 1))[: 3 * out_cols]
    out_back = group.exchange(grad_out)
    first_grad = jnp.concatenate(
        [grad_qkv[:, : 3 * out_cols], jnp.concatenate(out_back, axis=0)], axis=1
    )
    first_total = group.unshare(
        group.scatter(first_grad.reshape(groups, twins * rows, width)).reshape(twins, rows, width)
    )

    hidden = jnp.dot(normed_mlp, in_all, preferred_element_type=wide) + bias_in_own
    share_below = 0.5 + 0.5 * lax.erf(hidden * 0.5**0.5)
    act_half = (hidden * share_below).astype(half)
    grad_down = lax.dot_general(
        act_half, cot_flat, (((0,), (0,)), ((), ())), preferred_element_type=wide
    ).astype(half)
    down_total = group.from_replicas(
        group.scatter(grad_down.reshape(groups, units, D)).astype(half)
    )
    grad_act = lax.dot_general(
        cot_flat, down_all, (((1,), (1,)), ((), ())), preferred_element_type=wide
    )
    density = jnp.exp(-0.5 * hidden * hidden) * (2.0 * np.pi) ** -0.5
    grad_hidden = grad_act * (share_below + hidden * density)
    hidden_half = grad_hidden.astype(half)
    grad_in = lax.dot_general(
        normed_mlp, hidden_half, (((0,), (0,)), ((), ())), preferred_element_type=wide
    ).astype(half)
    partial_mlp = lax.dot_general(
        hidden_half, in_all, (((1,), (1,)), ((), ())), preferred_element_type=wide
    )
    partial_out = branch_attn + jnp.dot(act_half, down_all, preferred_element_type=wide)
    branch = group.reduce_sequences(partial_out.reshape(seqs, length, D))
    output = (tokens.astype(wide) + branch + (bias_out + bias_down)).astype(half)

    partial_slope = partial_attn * gain_one + partial_mlp * gain_two
    own = batch * length
    own_unit = unit[:own]
    own_cot = cotangent.reshape(own, D).astype(wide)
    slope = group.reduce_sequences(partial_slope.reshape(seqs, length, D)).reshape(own, D)
    scale = lax.rsqrt(spread[:own] + norm_eps)
    back = scale * (
        slope
        - jnp.mean(slope, axis=-1, keepdims=True)
        - own_unit * jnp.mean(slope * own_unit, axis=-1, keepdims=True)
    )
    input_grad = (own_cot + back).reshape(batch, length, D)

    def columns(values, outer):
        zero = jnp.zeros((outer, ways, values.shape[0] // outer), wide)
        return lax.dynamic_update_slice(
            zero, values.reshape(outer, 1, -1), (0, group.rank, 0)
        ).reshape(-1)

    column_sum = jnp.sum(own_cot, axis=0)
    vector_grad = jnp.concatenate(
        [
            jnp.sum(partial_attn * unit, axis=0),
            jnp.sum(partial_attn, axis=0),
            jnp.sum(partial_mlp * unit, axis=0),
            jnp.sum(partial_mlp, axis=0),
            columns(bias_qkv_grad, 3),
            column_sum,
            columns(jnp.sum(grad_hidden, axis=0), groups),
            column_sum,
        ]
    ).reshape(groups, twins, vec_size)
    vector_grad = jnp.pad(
        vector_grad.astype(half), ((0, 0), (0, 0), (0, vec_rows * width - vec_size))
    ).reshape(groups, twins, vec_rows, width)
    in_grad = jnp.concatenate([grad_in.reshape(groups, twins, rows, width), vector_grad], axis=2)
    in_total = group.unshare(group.scatter(in_grad, 2))
    vec_total = jnp.sum(in_total[:, rows:].astype(wide), axis=0).reshape(-1)[:vec_size]

    totals = (
        first_total[:, :, : 3 * out_cols]
        .reshape(ways, rows, 3, out_cols)
        .transpose(1, 2, 0, 3)
        .reshape(rows, -1)
        .astype(wide),
        first_total[:, :, 3 * out_cols :].transpose(1, 0, 2).reshape(rows, -1).astype(wide),
        in_total[:, :rows]
        .reshape(ways, rows, groups, units)
        .transpose(1, 2, 0, 3)
        .reshape(rows, -1)
        .astype(wide),
        down_total.reshape(-1, D).astype(wide),
        vec_total,
    )
    masters = (w_qkv, w_out, w_in, w_down, vectors)
    firsts = (m_qkv, m_out, m_in, m_down, m_vec)
    seconds = (v_qkv, v_out, v_in, v_down, v_vec)
    decays = (decay_rate, decay_rate, decay_rate, decay_rate, 0.0)
    results = [
        adamw(masters[number], totals[number], firsts[number], seconds[number], decays[number])
        for number in range(5)
    ]
    return (
        output,
        input_grad,
        *totals,
        *(result[0] for result in results),
        *(result[1] for result in results),
        *(result[2] for result in results),
    )


def solution(mesh):
    placed = (
        P(("shard", "replica"), None, None),
        P(("shard", "replica"), None),
        P(("shard", "replica"), None, None),
        P("shard", None),
        P("shard", None),
        P("shard", None),
        P("shard", None),
        P("shard"),
        P("shard", None),
        P("shard", None),
        P("shard", None),
        P("shard", None),
        P("shard"),
        P("shard", None),
        P("shard", None),
        P("shard", None),
        P("shard", None),
        P("shard"),
    )
    return jax.shard_map(
        functools.partial(body, Group(mesh)),
        mesh=mesh,
        in_specs=placed,
        out_specs=(
            P(("shard", "replica"), None, None),
            P(("shard", "replica"), None, None),
            P("shard", None),
            P("shard", None),
            P("shard", None),
            P("shard", None),
            P("shard"),
            P("shard", None),
            P("shard", None),
            P("shard", None),
            P("shard", None),
            P("shard"),
            P("shard", None),
            P("shard", None),
            P("shard", None),
            P("shard", None),
            P("shard"),
            P("shard", None),
            P("shard", None),
            P("shard", None),
            P("shard", None),
            P("shard"),
        ),
        check_vma=False,
    )
```

```python
import functools

import jax
import jax.numpy as jnp
import numpy as np
from jax import lax
from jax.experimental import pallas as pl
from jax.experimental.pallas import tpu as pltpu
from jax.sharding import PartitionSpec as P

D = 768
HEADS = 12
HEAD_DIM = 64
FF = 3072
ROT = 16
STEP = 5


norm_eps = 1e-05
learn_rate = 0.01
beta_first = 0.9
beta_second = 0.999
adam_eps = 1e-08
decay_rate = 0.1


def split_vectors(vectors):
    bounds = [0, D, 2 * D, 3 * D, 4 * D, 7 * D, 8 * D, 8 * D + FF, 9 * D + FF]
    return [vectors[bounds[number] : bounds[number + 1]] for number in range(8)]


def rotary_lanes(length, heads):
    half_rot = ROT // 2
    freqs = 10000.0 ** (-np.arange(half_rot) * 2.0 / ROT)
    angles = np.arange(length)[:, None] * freqs[None, :]
    cosine = np.ones((length, HEAD_DIM))
    sine = np.zeros((length, HEAD_DIM))
    cosine[:, :ROT] = np.tile(np.cos(angles), (1, 2))
    sine[:, :ROT] = np.tile(np.sin(angles), (1, 2))
    partner = np.zeros((HEAD_DIM, HEAD_DIM))
    for lane in range(half_rot):
        partner[lane + half_rot, lane] = -1.0
        partner[lane, lane + half_rot] = 1.0
    cosine = jnp.tile(jnp.asarray(cosine, jnp.float32), (1, heads))
    sine = jnp.tile(jnp.asarray(sine, jnp.float32), (1, heads))
    return cosine, sine, jnp.asarray(np.kron(np.eye(heads), partner), jnp.bfloat16)


def contract(left, right, left_dim, right_dim):
    return lax.dot_general(
        left, right, (((left_dim,), (right_dim,)), ((), ())), preferred_element_type=jnp.float32
    )


def attention_kernel(
    ways,
    heads,
    normed_ref,
    cot_ref,
    seg_col_ref,
    seg_row_ref,
    qkv_ref,
    out_ref,
    bias_ref,
    cos_ref,
    sin_ref,
    partner_ref,
    mixed_ref,
    branch_ref,
    slope_ref,
    sums_ref,
    grad_qkv_ref,
    grad_out_ref,
    qkv_total,
    out_total,
):
    half = jnp.bfloat16
    wide = jnp.float32
    step = pl.program_id(0)
    cols = heads * HEAD_DIM
    cosine, sine, partner = cos_ref[...], sin_ref[...], partner_ref[...]

    def partners(values):
        high = values.astype(half)
        low = (values - high.astype(wide)).astype(half)
        return contract(high, partner, 1, 0) + contract(low, partner, 1, 0)

    normed = normed_ref[...]
    cot = cot_ref[...]
    projected = contract(normed, qkv_ref[...], 1, 0) + bias_ref[...]
    query, keyed = projected[:, :cols], projected[:, cols : 2 * cols]
    query = (query * cosine + partners(query) * sine).astype(half)
    keyed = (keyed * cosine + partners(keyed) * sine).astype(half)
    valued = projected[:, 2 * cols : 3 * cols].astype(half)
    grad_mixed = contract(cot, out_ref[...], 1, 1).astype(half)
    length = normed.shape[0]
    row = lax.broadcasted_iota(jnp.int32, (length, length), 0)
    column = lax.broadcasted_iota(jnp.int32, (length, length), 1)
    allowed = (seg_col_ref[0] == seg_row_ref[0]) & (row >= column)
    mixed, grad_q, grad_k, grad_v = [], [], [], []
    for head in range(heads):
        lanes = slice(head * HEAD_DIM, (head + 1) * HEAD_DIM)
        q, k, v, g = query[:, lanes], keyed[:, lanes], valued[:, lanes], grad_mixed[:, lanes]
        scores = jnp.where(allowed, contract(q, k, 1, 1) * HEAD_DIM ** (-0.5), -1e30)
        shifted = jnp.exp(scores - jnp.max(scores, axis=1, keepdims=True))
        probs_full = shifted / jnp.sum(shifted, axis=1, keepdims=True)
        probs = probs_full.astype(half)
        mixed.append(contract(probs, v, 1, 0))
        grad_v.append(contract(probs, g, 0, 0))
        grad_probs = contract(g, v, 1, 1)
        inner = jnp.sum(probs_full * grad_probs, axis=1, keepdims=True)
        grad_scores = (probs_full * (grad_probs - inner) * HEAD_DIM ** (-0.5)).astype(half)
        grad_q.append(contract(grad_scores, k, 1, 0))
        grad_k.append(contract(grad_scores, q, 0, 0))
    mixed = jnp.concatenate(mixed, axis=1).astype(half)
    grad_q = jnp.concatenate(grad_q, axis=1)
    grad_k = jnp.concatenate(grad_k, axis=1)
    grad_v = jnp.concatenate(grad_v, axis=1)
    grad_q = grad_q * cosine - partners(grad_q) * sine
    grad_k = grad_k * cosine - partners(grad_k) * sine
    grad_projected = jnp.concatenate([grad_q, grad_k, grad_v, jnp.zeros_like(grad_v)], axis=1)
    projected_half = grad_projected.astype(half)
    sums_ref[0] = jnp.sum(grad_projected, axis=0, keepdims=True)
    mixed_ref[...] = mixed
    branch_ref[...] = contract(mixed, out_ref[...], 1, 0)
    slope_ref[...] = contract(projected_half, qkv_ref[...], 1, 1)

    @pl.when(step == 0)
    def _():
        qkv_total[...] = jnp.zeros_like(qkv_total)
        out_total[...] = jnp.zeros_like(out_total)

    qkv_total[...] += contract(normed, projected_half, 0, 0)
    out_total[...] += contract(mixed, cot, 0, 0)

    @pl.when(step == pl.num_programs(0) - 1)
    def _():
        grad_qkv_ref[...] = qkv_total[...].astype(half)
        for way in range(ways):
            grad_out_ref[way] = out_total[:, way * cols : (way + 1) * cols].astype(half)


def attention(normed, cot, seg, qkv_all, out_all, bias, ways, heads):
    half = jnp.bfloat16
    wide = jnp.float32
    seqs, length = seg.shape
    count = seqs * length
    cols = heads * HEAD_DIM
    width = qkv_all.shape[1]
    cosine, sine, partner = rotary_lanes(length, heads)
    bias_row = jnp.pad(bias, (0, width - 3 * cols))[None]

    def block(rows, lanes):
        return pl.BlockSpec((rows, lanes), lambda s: (s, 0))

    def whole(*shape):
        return pl.BlockSpec(shape, lambda s: (0,) * len(shape))

    flops = 2 * count * (2 * D * width * 2 + 3 * D * cols + 7 * length * cols)
    return pl.pallas_call(
        functools.partial(attention_kernel, ways, heads),
        grid=(seqs,),
        in_specs=[
            block(length, D),
            block(length, D),
            pl.BlockSpec((1, length, 1), lambda s: (s, 0, 0)),
            pl.BlockSpec((1, 1, length), lambda s: (s, 0, 0)),
            whole(D, width),
            whole(cols, D),
            whole(1, width),
            whole(length, cols),
            whole(length, cols),
            whole(cols, cols),
        ],
        out_specs=[
            block(length, cols),
            block(length, D),
            block(length, D),
            pl.BlockSpec((1, 1, width), lambda s: (s, 0, 0)),
            whole(D, width),
            whole(ways, cols, cols),
        ],
        out_shape=[
            jax.ShapeDtypeStruct((count, cols), half),
            jax.ShapeDtypeStruct((count, D), wide),
            jax.ShapeDtypeStruct((count, D), wide),
            jax.ShapeDtypeStruct((seqs, 1, width), wide),
            jax.ShapeDtypeStruct((D, width), half),
            jax.ShapeDtypeStruct((ways, cols, cols), half),
        ],
        scratch_shapes=[pltpu.VMEM((D, width), wide), pltpu.VMEM((cols, D), wide)],
        compiler_params=pltpu.CompilerParams(dimension_semantics=("arbitrary",)),
        cost_estimate=pl.CostEstimate(
            flops=flops, bytes_accessed=18 * 1024 * 1024, transcendentals=seqs * heads * length**2
        ),
        name="attention_block",
    )(
        normed,
        cot,
        seg[:, :, None],
        seg[:, None, :],
        qkv_all,
        out_all,
        bias_row,
        cosine,
        sine,
        partner,
    )


class Group:
    def __init__(self, mesh):
        self.shards = mesh.shape["shard"]
        self.replicas = mesh.shape["replica"]
        self.rings = self.shards <= 16 and self.shards % 4 == 0
        self.twins = 2 if self.rings and HEADS % (2 * self.replicas) == 0 else 1
        self.ways = self.twins * self.replicas
        self.groups = self.shards // self.twins
        self.pairs = 2 if self.groups % 2 == 0 else 1
        self.lines = self.groups // self.pairs

    def place(self):
        shard = lax.axis_index("shard")
        self.twin = shard % self.twins
        self.group = shard // self.twins
        self.pair = self.group % self.pairs
        self.line = self.group // self.pairs
        self.replica = lax.axis_index("replica")
        self.rank = self.twin * self.replicas + self.replica


    def from_twin(self, array):
        return lax.ppermute(array, "shard", [(s, s ^ 1) for s in range(self.shards)])

    def from_pair(self, array):
        step = self.twins
        return lax.ppermute(array, "shard", [(s, s ^ step) for s in range(self.shards)])

    def along_line(self, array, hops):
        block = self.twins * self.pairs
        return lax.ppermute(
            array,
            "shard",
            [
                (s, ((s // block + hops) % self.lines) * block + s % block)
                for s in range(self.shards)
            ],
        )

    def to_replica(self, array, hops):
        size = self.replicas
        return lax.ppermute(array, "replica", [(c, (c + hops) % size) for c in range(size)])

    def twins_in_order(self, own, far):
        return jnp.stack(
            [jnp.where(self.twin == 0, own, far), jnp.where(self.twin == 0, far, own)]
        )

    def to_rank(self, array, twin_flip, hops):
        size = self.replicas
        pairs = [
            (s * size + c, (s ^ twin_flip) * size + (c + hops) % size)
            for s in range(self.shards)
            for c in range(size)
        ]
        return lax.ppermute(array, ("shard", "replica"), pairs)


    def gather_whole(self, piece):
        members = None
        if self.twins > 1:
            members = [
                [group * self.twins + twin for group in range(self.groups)]
                for twin in range(self.twins)
            ]
        return lax.all_gather(piece, "shard", axis=0, tiled=False, axis_index_groups=members)

    def gather(self, piece):
        if not self.rings:
            return self.gather_whole(piece)
        held = [piece]
        for hops in range(1, self.lines):
            held.append(self.along_line(piece, hops))
        buffer = jnp.zeros((self.groups,) + piece.shape, piece.dtype)
        zeros = (0,) * piece.ndim
        for hops, block in enumerate(held):
            line = (self.line - hops) % self.lines
            own = line * self.pairs + self.pair
            buffer = lax.dynamic_update_slice(buffer, block[None], (own,) + zeros)
        for hops, block in enumerate(held):
            line = (self.line - hops) % self.lines
            other = line * self.pairs + (self.pair ^ 1)
            buffer = lax.dynamic_update_slice(
                buffer, self.from_pair(block)[None], (other,) + zeros
            )
        return buffer

    def scatter(self, terms, pieces=1, marks=None, before=()):
        wide = jnp.float32
        if not self.rings:
            total = lax.psum_scatter(terms.astype(wide), "shard", scatter_dimension=0, tiled=False)
            return total
        halves = terms.reshape((self.lines, self.pairs) + terms.shape[1:])
        keep = lax.dynamic_index_in_dim(halves, self.pair, 1, keepdims=False)
        give = lax.dynamic_index_in_dim(halves, self.pair ^ 1, 1, keepdims=False)

        def block(array, hops):
            return lax.dynamic_index_in_dim(
                array, (self.line + hops) % self.lines, 0, keepdims=False
            )

        order = [hops for hops in range(1, self.lines)] + [0]
        if pieces == 1:
            merged = keep.astype(wide) + self.from_pair(give).astype(wide)
            if before:
                merged = after(merged, *before)
            if marks is not None:
                marks.append(merged)
            sums = {hops: block(merged, hops) for hops in order}
        else:
            sums = {}
            size = -(-self.lines // pieces)
            for start in range(0, self.lines, size):
                chosen = order[start : start + size]
                far = self.from_pair(jnp.stack([block(give, hops) for hops in chosen]))
                if before:
                    far = after(far, *before)
                for place, hops in enumerate(chosen):
                    sums[hops] = block(keep, hops).astype(wide) + far[place].astype(wide)
        total = sums[0]
        for hops in range(1, self.lines):
            total = total + self.along_line(sums[hops].astype(jnp.bfloat16), hops).astype(wide)
        return total

    def gather_sequences(self, array):
        across = array[None]
        if self.twins == 2:
            across = jnp.stack([array, self.from_twin(array)])
        slots = [across]
        for hops in range(1, self.replicas):
            slots.append(self.to_replica(across, self.replicas - hops))
        return jnp.stack(slots).reshape((-1,) + array.shape[1:])

    def reduce_sequences(self, partial, marks=None):
        wire = jnp.bfloat16
        wide = jnp.float32
        shape = partial.shape
        batch = shape[0] // self.ways
        slots = partial.reshape((self.replicas, self.twins, batch) + shape[1:])
        total = slots[0]
        for hops in range(1, self.replicas):
            total = total + self.to_replica(slots[hops].astype(wire), hops).astype(wide)
        own = total[0]
        if self.twins == 2:
            give = total[1].astype(wire)
            if marks is not None:
                marks.append(give)
            own = own + self.from_twin(give).astype(wide)
        return own


    def share(self, pick):
        own = pick(self.rank)
        if self.twins == 1:
            return own[None]
        far = self.from_twin(pick((self.twin ^ 1) * self.replicas + self.replica))
        return self.twins_in_order(own, far)

    def from_replicas(self, own):
        held = [own] + [self.to_replica(own, hops) for hops in range(1, self.replicas)]
        if self.replicas == 2:
            return jnp.stack(
                [
                    jnp.where(self.replica == 0, held[0], held[1]),
                    jnp.where(self.replica == 0, held[1], held[0]),
                ]
            )
        result = jnp.zeros((self.replicas,) + own.shape, own.dtype)
        for hops, part in enumerate(held):
            source = (self.replica - hops) % self.replicas
            result = lax.dynamic_update_slice(result, part[None], (source,) + (0,) * own.ndim)
        return result

    def unshare(self, rows):
        half = jnp.bfloat16
        own = lax.dynamic_index_in_dim(rows, self.twin, 0, keepdims=False).astype(half)
        if self.twins == 2:
            give = lax.dynamic_index_in_dim(rows, self.twin ^ 1, 0, keepdims=False)
            both = self.twins_in_order(own, self.from_twin(give.astype(half)))
        else:
            both = own[None]
        stacked = jnp.swapaxes(self.from_replicas(both), 0, 1)
        return stacked.reshape((self.ways,) + own.shape)

    def routes(self):
        pairs = []
        for holder in range(self.shards * self.replicas):
            rank, group = holder // self.groups, holder % self.groups
            shard = group * self.twins + rank // self.replicas
            pairs.append((holder, shard * self.replicas + rank % self.replicas))
        return pairs

    def to_users(self, piece):
        return lax.ppermute(piece, ("shard", "replica"), self.routes())

    def to_holders(self, piece):
        back = [(user, holder) for holder, user in self.routes()]
        return lax.ppermute(piece, ("shard", "replica"), back)


def after(value, *earlier):
    return lax.optimization_barrier((value, *earlier))[0]


def adamw(weight, gradient, moment_one, moment_two, decay_on):
    moment_one = beta_first * moment_one + (1.0 - beta_first) * gradient
    moment_two = beta_second * moment_two + (1.0 - beta_second) * gradient * gradient
    first_hat = moment_one / (1.0 - beta_first**STEP)
    second_hat = moment_two / (1.0 - beta_second**STEP)
    updated = weight - learn_rate * (
        first_hat / (jnp.sqrt(second_hat) + adam_eps) + decay_on * weight
    )
    return (updated, moment_one, moment_two)


def step(
    group,
    tokens,
    segment_ids,
    cotangent,
    w_qkv,
    w_out,
    w_in,
    w_down,
    vectors,
    m_qkv,
    m_out,
    m_in,
    m_down,
    m_vec,
    v_qkv,
    v_out,
    v_in,
    v_down,
    v_vec,
):
    group.place()
    half = jnp.bfloat16
    wide = jnp.float32
    ways = group.ways
    groups = group.groups
    twins = group.twins
    heads = HEADS // ways
    rows = w_qkv.shape[0]
    units = FF // (groups * ways)
    out_cols = D // ways
    width = 4 * out_cols
    batch, length = tokens.shape[:2]
    seqs = batch * ways
    count = seqs * length
    vec_size = vectors.shape[0]
    vec_rows = -(-vec_size // (8 * width)) * 8

    qkv_half = w_qkv.astype(half).reshape(rows, 3, ways, out_cols)
    in_half = w_in.astype(half).reshape(rows, groups, ways, units)
    down_half = w_down.astype(half).reshape(group.replicas, units, D)
    vec_half = jnp.pad(vectors.astype(half), (0, vec_rows * width - vec_size))
    vec_half = vec_half.reshape(vec_rows, width)
    out_rows = rows // group.replicas
    out_half = lax.dynamic_slice_in_dim(w_out, group.replica * out_rows, out_rows, 0)
    out_piece = group.to_users(out_half.astype(half))
    out_piece = out_piece.reshape(out_rows, ways, out_cols).transpose(1, 0, 2)

    def pick(rank):
        qkv = lax.dynamic_index_in_dim(qkv_half, rank, 2, keepdims=False).reshape(rows, -1)
        qkv = jnp.concatenate([qkv, jnp.zeros((rows, out_cols), half)], axis=1)
        into = lax.dynamic_index_in_dim(in_half, rank, 2, keepdims=False).reshape(rows, -1)
        return jnp.concatenate([qkv, vec_half, into], axis=0)

    shared = group.share(pick)
    down_piece = lax.dynamic_index_in_dim(down_half, group.replica, 0, keepdims=False)
    second_piece = jnp.concatenate(
        [shared[:, rows + vec_rows :].reshape(-1, width), down_piece.reshape(-1, width)], axis=0
    )
    second = group.gather_whole(second_piece)
    first_piece = lax.dynamic_update_slice(
        shared[:, : rows + vec_rows],
        out_piece.reshape(twins, rows, out_cols),
        (0, 0, 3 * out_cols),
    )

    seg_rows = jnp.pad(segment_ids.astype(half)[:, None], ((0, 0), (0, 7), (0, D - length)))
    pack = jnp.concatenate([tokens, cotangent, seg_rows], axis=1)
    packs = group.gather_sequences(after(pack, shared))
    x_seqs = packs[:, :length]
    cot = packs[:, length : 2 * length]
    seg = packs[:, 2 * length, :length].astype(wide)

    first = group.gather(first_piece)
    qkv_all = first[:, :, :rows].reshape(D, width)
    vec_all = first[:, :, rows:].reshape(group.shards, -1)[:, :vec_size].reshape(-1).astype(wide)
    in_all = second[:, : twins * rows].reshape(D, width)
    down_all = second[:, twins * rows :].reshape(width, D)
    out_all = first[:, :, :rows, 3 * out_cols :].reshape(groups, ways, out_rows, out_cols)
    out_all = out_all.transpose(0, 2, 1, 3).reshape(out_cols, D)

    gain_one, offset_one, gain_two, offset_two, bias_qkv, bias_out, bias_in, bias_down = (
        split_vectors(vec_all)
    )
    bias_qkv_own = lax.dynamic_index_in_dim(
        bias_qkv.reshape(3, ways, -1), group.rank, 1, keepdims=False
    ).reshape(-1)
    bias_in_own = lax.dynamic_index_in_dim(
        bias_in.reshape(groups, ways, units), group.rank, 1, keepdims=False
    ).reshape(-1)

    inputs = x_seqs.reshape(count, D).astype(wide)
    center = inputs - jnp.mean(inputs, axis=-1, keepdims=True)
    spread = jnp.mean(center * center, axis=-1, keepdims=True)
    unit = center * lax.rsqrt(spread + norm_eps)
    normed_attn = (unit * gain_one + offset_one).astype(half)
    normed_mlp = (unit * gain_two + offset_two).astype(half)
    cot_flat = cot.reshape(count, D)
    _, branch_attn, partial_attn, sums_attn, grad_qkv, grad_out = attention(
        normed_attn, cot_flat, seg, qkv_all, out_all, bias_qkv_own, ways, heads
    )
    bias_qkv_grad = jnp.sum(sums_attn, axis=(0, 1))[: 3 * out_cols]
    out_back = grad_out.reshape(ways, groups, out_rows, out_cols).transpose(1, 0, 2, 3)
    first_grad = jnp.concatenate(
        [
            grad_qkv[:, : 3 * out_cols].reshape(groups, twins * rows, -1),
            out_back.reshape(groups, twins * rows, out_cols),
        ],
        axis=2,
    )
    marks = []
    first_sum = group.scatter(first_grad, 1, marks)
    first_total = group.unshare(first_sum[:, : 3 * out_cols].reshape(twins, rows, -1))
    out_sum = first_sum[:, 3 * out_cols :].astype(half).reshape(ways, out_rows, out_cols)
    out_sum = out_sum.transpose(1, 0, 2).reshape(out_rows, D)
    out_total = group.from_replicas(group.to_holders(out_sum)).reshape(rows, D)

    hidden = jnp.dot(normed_mlp, in_all, preferred_element_type=wide) + bias_in_own
    share_below = 0.5 + 0.5 * lax.erf(hidden * 0.5**0.5)
    act_half = (hidden * share_below).astype(half)
    grad_down = lax.dot_general(
        act_half, cot_flat, (((0,), (0,)), ((), ())), preferred_element_type=wide
    ).astype(half)
    sent = []
    grad_act = lax.dot_general(
        after(cot_flat, grad_down, *marks), down_all, (((1,), (1,)), ((), ())), preferred_element_type=wide
    )
    density = jnp.exp(-0.5 * hidden * hidden) * (2.0 * np.pi) ** -0.5
    grad_hidden = grad_act * (share_below + hidden * density)
    hidden_half = grad_hidden.astype(half)
    grad_in = lax.dot_general(
        normed_mlp, hidden_half, (((0,), (0,)), ((), ())), preferred_element_type=wide
    ).astype(half)
    partial_mlp = lax.dot_general(
        hidden_half, in_all, (((1,), (1,)), ((), ())), preferred_element_type=wide
    )
    partial_out = branch_attn + jnp.dot(act_half, down_all, preferred_element_type=wide)
    branch = group.reduce_sequences(partial_out.reshape(seqs, length, D), sent)
    output = (tokens.astype(wide) + branch + (bias_out + bias_down)).astype(half)

    partial_slope = partial_attn * gain_one + partial_mlp * gain_two
    own = batch * length
    own_unit = unit[:own]
    own_cot = cotangent.reshape(own, D).astype(wide)
    slope = group.reduce_sequences(partial_slope.reshape(seqs, length, D), sent).reshape(own, D)
    down_total = group.from_replicas(
        group.scatter(grad_down.reshape(groups, units, D), before=sent[:1]).astype(half)
    )
    scale = lax.rsqrt(spread[:own] + norm_eps)
    back = scale * (
        slope
        - jnp.mean(slope, axis=-1, keepdims=True)
        - own_unit * jnp.mean(slope * own_unit, axis=-1, keepdims=True)
    )
    input_grad = (own_cot + back).reshape(batch, length, D)

    def columns(values, outer):
        zero = jnp.zeros((outer, ways, values.shape[0] // outer), wide)
        return lax.dynamic_update_slice(
            zero, values.reshape(outer, 1, -1), (0, group.rank, 0)
        ).reshape(-1)

    column_sum = jnp.sum(own_cot, axis=0)
    vector_grad = jnp.concatenate(
        [
            jnp.sum(partial_attn * unit, axis=0),
            jnp.sum(partial_attn, axis=0),
            jnp.sum(partial_mlp * unit, axis=0),
            jnp.sum(partial_mlp, axis=0),
            columns(bias_qkv_grad, 3),
            column_sum,
            columns(jnp.sum(grad_hidden, axis=0), groups),
            column_sum,
        ]
    ).reshape(groups, twins, vec_size)
    vector_grad = jnp.pad(
        vector_grad.astype(half), ((0, 0), (0, 0), (0, vec_rows * width - vec_size))
    ).reshape(groups, twins, vec_rows, width)
    in_grad = jnp.concatenate([grad_in.reshape(groups, twins, rows, width), vector_grad], axis=2)
    in_total = group.unshare(group.scatter(in_grad, 2, before=sent))
    vec_total = jnp.sum(in_total[:, rows:].astype(wide), axis=0).reshape(-1)[:vec_size]

    totals = (
        first_total.reshape(ways, rows, 3, out_cols)
        .transpose(1, 2, 0, 3)
        .reshape(rows, -1)
        .astype(wide),
        out_total.astype(wide),
        in_total[:, :rows]
        .reshape(ways, rows, groups, units)
        .transpose(1, 2, 0, 3)
        .reshape(rows, -1)
        .astype(wide),
        down_total.reshape(-1, D).astype(wide),
        vec_total,
    )
    masters = (w_qkv, w_out, w_in, w_down, vectors)
    firsts = (m_qkv, m_out, m_in, m_down, m_vec)
    seconds = (v_qkv, v_out, v_in, v_down, v_vec)
    decays = (decay_rate, decay_rate, decay_rate, decay_rate, 0.0)
    results = [
        adamw(masters[number], totals[number], firsts[number], seconds[number], decays[number])
        for number in range(5)
    ]
    return (
        output,
        input_grad,
        *totals,
        *(result[0] for result in results),
        *(result[1] for result in results),
        *(result[2] for result in results),
    )


def solution(mesh):
    placed = (
        P(("shard", "replica"), None, None),
        P(("shard", "replica"), None),
        P(("shard", "replica"), None, None),
        P("shard", None),
        P("shard", None),
        P("shard", None),
        P("shard", None),
        P("shard"),
        P("shard", None),
        P("shard", None),
        P("shard", None),
        P("shard", None),
        P("shard"),
        P("shard", None),
        P("shard", None),
        P("shard", None),
        P("shard", None),
        P("shard"),
    )
    return jax.shard_map(
        functools.partial(step, Group(mesh)),
        mesh=mesh,
        in_specs=placed,
        out_specs=(
            P(("shard", "replica"), None, None),
            P(("shard", "replica"), None, None),
            P("shard", None),
            P("shard", None),
            P("shard", None),
            P("shard", None),
            P("shard"),
            P("shard", None),
            P("shard", None),
            P("shard", None),
            P("shard", None),
            P("shard"),
            P("shard", None),
            P("shard", None),
            P("shard", None),
            P("shard", None),
            P("shard"),
            P("shard", None),
            P("shard", None),
            P("shard", None),
            P("shard", None),
            P("shard"),
        ),
        check_vma=False,
    )
```

```python
import functools

import jax
import jax.numpy as jnp
import numpy as np
from jax import lax
from jax.experimental import pallas as pl
from jax.experimental.pallas import tpu as pltpu
from jax.sharding import PartitionSpec as P

D = 768
HEADS = 12
HEAD_DIM = 64
FF = 3072
ROT = 16
STEP = 5


norm_eps = 1e-05
learn_rate = 0.01
beta_first = 0.9
beta_second = 0.999
adam_eps = 1e-08
decay_rate = 0.1


def split_vectors(vectors):
    bounds = [0, D, 2 * D, 3 * D, 4 * D, 7 * D, 8 * D, 8 * D + FF, 9 * D + FF]
    return [vectors[bounds[number] : bounds[number + 1]] for number in range(8)]


def rotary_lanes(length, heads):
    half_rot = ROT // 2
    freqs = 10000.0 ** (-np.arange(half_rot) * 2.0 / ROT)
    angles = np.arange(length)[:, None] * freqs[None, :]
    cosine = np.ones((length, HEAD_DIM))
    sine = np.zeros((length, HEAD_DIM))
    cosine[:, :ROT] = np.tile(np.cos(angles), (1, 2))
    sine[:, :ROT] = np.tile(np.sin(angles), (1, 2))
    partner = np.zeros((HEAD_DIM, HEAD_DIM))
    for lane in range(half_rot):
        partner[lane + half_rot, lane] = -1.0
        partner[lane, lane + half_rot] = 1.0
    cosine = jnp.tile(jnp.asarray(cosine, jnp.float32), (1, heads))
    sine = jnp.tile(jnp.asarray(sine, jnp.float32), (1, heads))
    return cosine, sine, jnp.asarray(np.kron(np.eye(heads), partner), jnp.bfloat16)


def contract(left, right, left_dim, right_dim):
    return lax.dot_general(
        left, right, (((left_dim,), (right_dim,)), ((), ())), preferred_element_type=jnp.float32
    )


def attention_kernel(
    ways,
    heads,
    normed_ref,
    cot_ref,
    seg_col_ref,
    seg_row_ref,
    qkv_ref,
    out_ref,
    bias_ref,
    cos_ref,
    sin_ref,
    partner_ref,
    mixed_ref,
    branch_ref,
    slope_ref,
    sums_ref,
    grad_qkv_ref,
    grad_out_ref,
    qkv_total,
    out_total,
):
    half = jnp.bfloat16
    wide = jnp.float32
    step = pl.program_id(0)
    cols = heads * HEAD_DIM
    cosine, sine, partner = cos_ref[...], sin_ref[...], partner_ref[...]

    def partners(values):
        high = values.astype(half)
        low = (values - high.astype(wide)).astype(half)
        return contract(high, partner, 1, 0) + contract(low, partner, 1, 0)

    normed = normed_ref[...]
    cot = cot_ref[...]
    projected = contract(normed, qkv_ref[...], 1, 0) + bias_ref[...]
    query, keyed = projected[:, :cols], projected[:, cols : 2 * cols]
    query = (query * cosine + partners(query) * sine).astype(half)
    keyed = (keyed * cosine + partners(keyed) * sine).astype(half)
    valued = projected[:, 2 * cols : 3 * cols].astype(half)
    grad_mixed = contract(cot, out_ref[...], 1, 1).astype(half)
    length = normed.shape[0]
    row = lax.broadcasted_iota(jnp.int32, (length, length), 0)
    column = lax.broadcasted_iota(jnp.int32, (length, length), 1)
    allowed = (seg_col_ref[0] == seg_row_ref[0]) & (row >= column)
    mixed, grad_q, grad_k, grad_v = [], [], [], []
    for head in range(heads):
        lanes = slice(head * HEAD_DIM, (head + 1) * HEAD_DIM)
        q, k, v, g = query[:, lanes], keyed[:, lanes], valued[:, lanes], grad_mixed[:, lanes]
        scores = jnp.where(allowed, contract(q, k, 1, 1) * HEAD_DIM ** (-0.5), -1e30)
        shifted = jnp.exp(scores - jnp.max(scores, axis=1, keepdims=True))
        probs_full = shifted / jnp.sum(shifted, axis=1, keepdims=True)
        probs = probs_full.astype(half)
        mixed.append(contract(probs, v, 1, 0))
        grad_v.append(contract(probs, g, 0, 0))
        grad_probs = contract(g, v, 1, 1)
        inner = jnp.sum(probs_full * grad_probs, axis=1, keepdims=True)
        grad_scores = (probs_full * (grad_probs - inner) * HEAD_DIM ** (-0.5)).astype(half)
        grad_q.append(contract(grad_scores, k, 1, 0))
        grad_k.append(contract(grad_scores, q, 0, 0))
    mixed = jnp.concatenate(mixed, axis=1).astype(half)
    grad_q = jnp.concatenate(grad_q, axis=1)
    grad_k = jnp.concatenate(grad_k, axis=1)
    grad_v = jnp.concatenate(grad_v, axis=1)
    grad_q = grad_q * cosine - partners(grad_q) * sine
    grad_k = grad_k * cosine - partners(grad_k) * sine
    grad_projected = jnp.concatenate([grad_q, grad_k, grad_v, jnp.zeros_like(grad_v)], axis=1)
    projected_half = grad_projected.astype(half)
    sums_ref[0] = jnp.sum(grad_projected, axis=0, keepdims=True)
    mixed_ref[...] = mixed
    branch_ref[...] = contract(mixed, out_ref[...], 1, 0)
    slope_ref[...] = contract(projected_half, qkv_ref[...], 1, 1)

    @pl.when(step == 0)
    def _():
        qkv_total[...] = jnp.zeros_like(qkv_total)
        out_total[...] = jnp.zeros_like(out_total)

    qkv_total[...] += contract(normed, projected_half, 0, 0)
    out_total[...] += contract(mixed, cot, 0, 0)

    @pl.when(step == pl.num_programs(0) - 1)
    def _():
        grad_qkv_ref[...] = qkv_total[...].astype(half)
        for way in range(ways):
            grad_out_ref[way] = out_total[:, way * cols : (way + 1) * cols].astype(half)


def attention(normed, cot, seg, qkv_all, out_all, bias, ways, heads):
    half = jnp.bfloat16
    wide = jnp.float32
    seqs, length = seg.shape
    count = seqs * length
    cols = heads * HEAD_DIM
    width = qkv_all.shape[1]
    cosine, sine, partner = rotary_lanes(length, heads)
    bias_row = jnp.pad(bias, (0, width - 3 * cols))[None]

    def block(rows, lanes):
        return pl.BlockSpec((rows, lanes), lambda s: (s, 0))

    def whole(*shape):
        return pl.BlockSpec(shape, lambda s: (0,) * len(shape))

    flops = 2 * count * (2 * D * width * 2 + 3 * D * cols + 7 * length * cols)
    return pl.pallas_call(
        functools.partial(attention_kernel, ways, heads),
        grid=(seqs,),
        in_specs=[
            block(length, D),
            block(length, D),
            pl.BlockSpec((1, length, 1), lambda s: (s, 0, 0)),
            pl.BlockSpec((1, 1, length), lambda s: (s, 0, 0)),
            whole(D, width),
            whole(cols, D),
            whole(1, width),
            whole(length, cols),
            whole(length, cols),
            whole(cols, cols),
        ],
        out_specs=[
            block(length, cols),
            block(length, D),
            block(length, D),
            pl.BlockSpec((1, 1, width), lambda s: (s, 0, 0)),
            whole(D, width),
            whole(ways, cols, cols),
        ],
        out_shape=[
            jax.ShapeDtypeStruct((count, cols), half),
            jax.ShapeDtypeStruct((count, D), wide),
            jax.ShapeDtypeStruct((count, D), wide),
            jax.ShapeDtypeStruct((seqs, 1, width), wide),
            jax.ShapeDtypeStruct((D, width), half),
            jax.ShapeDtypeStruct((ways, cols, cols), half),
        ],
        scratch_shapes=[pltpu.VMEM((D, width), wide), pltpu.VMEM((cols, D), wide)],
        compiler_params=pltpu.CompilerParams(dimension_semantics=("arbitrary",)),
        cost_estimate=pl.CostEstimate(
            flops=flops, bytes_accessed=18 * 1024 * 1024, transcendentals=seqs * heads * length**2
        ),
        name="attention_block",
    )(
        normed,
        cot,
        seg[:, :, None],
        seg[:, None, :],
        qkv_all,
        out_all,
        bias_row,
        cosine,
        sine,
        partner,
    )


class Group:
    def __init__(self, mesh):
        self.shards = mesh.shape["shard"]
        self.replicas = mesh.shape["replica"]
        self.rings = self.shards <= 16 and self.shards % 4 == 0
        self.twins = 2 if self.rings and HEADS % (2 * self.replicas) == 0 else 1
        self.ways = self.twins * self.replicas
        self.groups = self.shards // self.twins
        self.pairs = 2 if self.groups % 2 == 0 else 1
        self.lines = self.groups // self.pairs

    def place(self):
        shard = lax.axis_index("shard")
        self.twin = shard % self.twins
        self.group = shard // self.twins
        self.pair = self.group % self.pairs
        self.line = self.group // self.pairs
        self.replica = lax.axis_index("replica")
        self.rank = self.twin * self.replicas + self.replica


    def from_twin(self, array):
        return lax.ppermute(array, "shard", [(s, s ^ 1) for s in range(self.shards)])

    def from_pair(self, array):
        step = self.twins
        return lax.ppermute(array, "shard", [(s, s ^ step) for s in range(self.shards)])

    def along_line(self, array, hops):
        block = self.twins * self.pairs
        return lax.ppermute(
            array,
            "shard",
            [
                (s, ((s // block + hops) % self.lines) * block + s % block)
                for s in range(self.shards)
            ],
        )

    def to_replica(self, array, hops):
        size = self.replicas
        return lax.ppermute(array, "replica", [(c, (c + hops) % size) for c in range(size)])

    def twins_in_order(self, own, far):
        return jnp.stack(
            [jnp.where(self.twin == 0, own, far), jnp.where(self.twin == 0, far, own)]
        )

    def to_rank(self, array, twin_flip, hops):
        size = self.replicas
        pairs = [
            (s * size + c, (s ^ twin_flip) * size + (c + hops) % size)
            for s in range(self.shards)
            for c in range(size)
        ]
        return lax.ppermute(array, ("shard", "replica"), pairs)


    def gather_whole(self, piece):
        members = None
        if self.twins > 1:
            members = [
                [group * self.twins + twin for group in range(self.groups)]
                for twin in range(self.twins)
            ]
        return lax.all_gather(piece, "shard", axis=0, tiled=False, axis_index_groups=members)

    def gather(self, piece):
        if not self.rings:
            return self.gather_whole(piece)
        held = [piece]
        for hops in range(1, self.lines):
            held.append(self.along_line(piece, hops))
        buffer = jnp.zeros((self.groups,) + piece.shape, piece.dtype)
        zeros = (0,) * piece.ndim
        for hops, block in enumerate(held):
            line = (self.line - hops) % self.lines
            own = line * self.pairs + self.pair
            buffer = lax.dynamic_update_slice(buffer, block[None], (own,) + zeros)
        for hops, block in enumerate(held):
            line = (self.line - hops) % self.lines
            other = line * self.pairs + (self.pair ^ 1)
            buffer = lax.dynamic_update_slice(
                buffer, self.from_pair(block)[None], (other,) + zeros
            )
        return buffer

    def scatter(self, terms, pieces=1, marks=None, before=()):
        wide = jnp.float32
        if not self.rings:
            total = lax.psum_scatter(terms.astype(wide), "shard", scatter_dimension=0, tiled=False)
            return total
        halves = terms.reshape((self.lines, self.pairs) + terms.shape[1:])
        keep = lax.dynamic_index_in_dim(halves, self.pair, 1, keepdims=False)
        give = lax.dynamic_index_in_dim(halves, self.pair ^ 1, 1, keepdims=False)

        def block(array, hops):
            return lax.dynamic_index_in_dim(
                array, (self.line + hops) % self.lines, 0, keepdims=False
            )

        order = [hops for hops in range(1, self.lines)] + [0]
        if pieces == 1:
            far = self.from_pair(give)
            merged = keep.astype(wide) + far.astype(wide)
            if before:
                merged = after(merged, *before)
            if marks is not None:
                marks.append(merged)
            sums = {hops: block(merged, hops) for hops in order}
        else:
            sums = {}
            size = -(-self.lines // pieces)
            for start in range(0, self.lines, size):
                chosen = order[start : start + size]
                far = jnp.stack([block(give, hops) for hops in chosen])
                far = self.from_pair(far)
                if before:
                    far = after(far, *before)
                if marks is not None:
                    marks.append(far)
                for place, hops in enumerate(chosen):
                    term = block(keep, hops).astype(wide) + far[place].astype(wide)
                    sums[hops] = term.astype(jnp.bfloat16) if hops else term
        total = sums[0]
        for hops in range(1, self.lines):
            give = sums[hops].astype(jnp.bfloat16)
            far = self.along_line(give, hops)
            total = total + far.astype(wide)
        return total

    def gather_sequences(self, array):
        across = array[None]
        if self.twins == 2:
            across = jnp.stack([array, self.from_twin(array)])
        slots = [across]
        for hops in range(1, self.replicas):
            slots.append(self.to_replica(across, self.replicas - hops))
        return jnp.stack(slots).reshape((-1,) + array.shape[1:])

    def reduce_sequences(self, partial, marks=None):
        wire = jnp.bfloat16
        wide = jnp.float32
        shape = partial.shape
        batch = shape[0] // self.ways
        slots = partial.reshape((self.replicas, self.twins, batch) + shape[1:])
        total = slots[0]
        for hops in range(1, self.replicas):
            far = self.to_replica(slots[hops].astype(wire), hops)
            total = total + far.astype(wide)
        own = total[0]
        if self.twins == 2:
            give = total[1].astype(wire)
            if marks is not None:
                marks.append(give)
            far = self.from_twin(give)
            own = own + far.astype(wide)
        return own


    def share(self, pick):
        own = pick(self.rank)
        if self.twins == 1:
            return own[None]
        far = self.from_twin(pick((self.twin ^ 1) * self.replicas + self.replica))
        return self.twins_in_order(own, far)

    def from_replicas(self, own):
        held = [own] + [self.to_replica(own, hops) for hops in range(1, self.replicas)]
        if self.replicas == 2:
            return jnp.stack(
                [
                    jnp.where(self.replica == 0, held[0], held[1]),
                    jnp.where(self.replica == 0, held[1], held[0]),
                ]
            )
        result = jnp.zeros((self.replicas,) + own.shape, own.dtype)
        for hops, part in enumerate(held):
            source = (self.replica - hops) % self.replicas
            result = lax.dynamic_update_slice(result, part[None], (source,) + (0,) * own.ndim)
        return result

    def unshare(self, rows):
        half = jnp.bfloat16
        own = lax.dynamic_index_in_dim(rows, self.twin, 0, keepdims=False).astype(half)
        if self.twins == 2:
            give = lax.dynamic_index_in_dim(rows, self.twin ^ 1, 0, keepdims=False)
            both = self.twins_in_order(own, self.from_twin(give.astype(half)))
        else:
            both = own[None]
        stacked = jnp.swapaxes(self.from_replicas(both), 0, 1)
        return stacked.reshape((self.ways,) + own.shape)

    def routes(self):
        pairs = []
        for holder in range(self.shards * self.replicas):
            rank, group = holder // self.groups, holder % self.groups
            shard = group * self.twins + rank // self.replicas
            pairs.append((holder, shard * self.replicas + rank % self.replicas))
        return pairs

    def to_users(self, piece):
        return lax.ppermute(piece, ("shard", "replica"), self.routes())

    def to_holders(self, piece):
        back = [(user, holder) for holder, user in self.routes()]
        return lax.ppermute(piece, ("shard", "replica"), back)


def after(value, *earlier):
    return lax.optimization_barrier((value, *earlier))[0]


def adamw(weight, gradient, moment_one, moment_two, decay_on):
    moment_one = beta_first * moment_one + (1.0 - beta_first) * gradient
    moment_two = beta_second * moment_two + (1.0 - beta_second) * gradient * gradient
    first_hat = moment_one / (1.0 - beta_first**STEP)
    second_hat = moment_two / (1.0 - beta_second**STEP)
    updated = weight - learn_rate * (
        first_hat / (jnp.sqrt(second_hat) + adam_eps) + decay_on * weight
    )
    return (updated, moment_one, moment_two)


def step(
    group,
    tokens,
    segment_ids,
    cotangent,
    w_qkv,
    w_out,
    w_in,
    w_down,
    vectors,
    m_qkv,
    m_out,
    m_in,
    m_down,
    m_vec,
    v_qkv,
    v_out,
    v_in,
    v_down,
    v_vec,
):
    group.place()
    half = jnp.bfloat16
    wide = jnp.float32
    ways = group.ways
    groups = group.groups
    twins = group.twins
    heads = HEADS // ways
    rows = w_qkv.shape[0]
    units = FF // (groups * ways)
    out_cols = D // ways
    width = 4 * out_cols
    batch, length = tokens.shape[:2]
    seqs = batch * ways
    count = seqs * length
    vec_size = vectors.shape[0]
    vec_rows = -(-vec_size // (8 * width)) * 8

    qkv_half = w_qkv.astype(half).reshape(rows, 3, ways, out_cols)
    in_half = w_in.astype(half).reshape(rows, groups, ways, units)
    down_half = w_down.astype(half).reshape(group.replicas, units, D)
    vec_half = jnp.pad(vectors.astype(half), (0, vec_rows * width - vec_size))
    vec_half = vec_half.reshape(vec_rows, width)
    out_rows = rows // group.replicas
    out_half = lax.dynamic_slice_in_dim(w_out, group.replica * out_rows, out_rows, 0)
    out_piece = group.to_users(out_half.astype(half))
    out_piece = out_piece.reshape(out_rows, ways, out_cols).transpose(1, 0, 2)

    def pick(rank):
        qkv = lax.dynamic_index_in_dim(qkv_half, rank, 2, keepdims=False).reshape(rows, -1)
        qkv = jnp.concatenate([qkv, jnp.zeros((rows, out_cols), half)], axis=1)
        into = lax.dynamic_index_in_dim(in_half, rank, 2, keepdims=False).reshape(rows, -1)
        return jnp.concatenate([qkv, vec_half, into], axis=0)

    shared = group.share(pick)
    down_piece = lax.dynamic_index_in_dim(down_half, group.replica, 0, keepdims=False)
    second_piece = jnp.concatenate(
        [shared[:, rows + vec_rows :].reshape(-1, width), down_piece.reshape(-1, width)], axis=0
    )
    second = group.gather_whole(second_piece)
    first_piece = lax.dynamic_update_slice(
        shared[:, : rows + vec_rows],
        out_piece.reshape(twins, rows, out_cols),
        (0, 0, 3 * out_cols),
    )

    seg_rows = jnp.pad(segment_ids.astype(half)[:, None], ((0, 0), (0, 7), (0, D - length)))
    pack = jnp.concatenate([tokens, cotangent, seg_rows], axis=1)
    packs = group.gather_sequences(after(pack, shared))
    x_seqs = packs[:, :length]
    cot = packs[:, length : 2 * length]
    seg = packs[:, 2 * length, :length].astype(wide)

    first = group.gather(first_piece)
    qkv_all = first[:, :, :rows].reshape(D, width)
    vec_all = first[:, :, rows:].reshape(group.shards, -1)[:, :vec_size].reshape(-1).astype(wide)
    in_all = second[:, : twins * rows].reshape(D, width)
    down_all = second[:, twins * rows :].reshape(width, D)
    out_all = first[:, :, :rows, 3 * out_cols :].reshape(groups, ways, out_rows, out_cols)
    out_all = out_all.transpose(0, 2, 1, 3).reshape(out_cols, D)

    gain_one, offset_one, gain_two, offset_two, bias_qkv, bias_out, bias_in, bias_down = (
        split_vectors(vec_all)
    )
    bias_qkv_own = lax.dynamic_index_in_dim(
        bias_qkv.reshape(3, ways, -1), group.rank, 1, keepdims=False
    ).reshape(-1)
    bias_in_own = lax.dynamic_index_in_dim(
        bias_in.reshape(groups, ways, units), group.rank, 1, keepdims=False
    ).reshape(-1)

    inputs = x_seqs.reshape(count, D).astype(wide)
    center = inputs - jnp.mean(inputs, axis=-1, keepdims=True)
    spread = jnp.mean(center * center, axis=-1, keepdims=True)
    unit = center * lax.rsqrt(spread + norm_eps)
    normed_attn = (unit * gain_one + offset_one).astype(half)
    normed_mlp = (unit * gain_two + offset_two).astype(half)
    cot_flat = cot.reshape(count, D)
    _, branch_attn, partial_attn, sums_attn, grad_qkv, grad_out = attention(
        normed_attn, cot_flat, seg, qkv_all, out_all, bias_qkv_own, ways, heads
    )
    bias_qkv_grad = jnp.sum(sums_attn, axis=(0, 1))[: 3 * out_cols]
    out_back = grad_out.reshape(ways, groups, out_rows, out_cols).transpose(1, 0, 2, 3)
    first_grad = jnp.concatenate(
        [
            grad_qkv[:, : 3 * out_cols].reshape(groups, twins * rows, -1),
            out_back.reshape(groups, twins * rows, out_cols),
        ],
        axis=2,
    )
    marks = []
    first_sum = group.scatter(first_grad, 1, marks)
    hidden = jnp.dot(normed_mlp, in_all, preferred_element_type=wide) + bias_in_own
    share_below = 0.5 + 0.5 * lax.erf(hidden * 0.5**0.5)
    act_half = (hidden * share_below).astype(half)
    grad_down = lax.dot_general(
        act_half, cot_flat, (((0,), (0,)), ((), ())), preferred_element_type=wide
    ).astype(half)
    sent = []
    back_cot = after(cot_flat, grad_down, *marks)
    grad_act = contract(back_cot, down_all, 1, 1)
    density = jnp.exp(-0.5 * hidden * hidden) * (2.0 * np.pi) ** -0.5
    grad_hidden = grad_act * (share_below + hidden * density)
    hidden_half = grad_hidden.astype(half)
    grad_in = lax.dot_general(
        normed_mlp, hidden_half, (((0,), (0,)), ((), ())), preferred_element_type=wide
    ).astype(half)
    partial_mlp = lax.dot_general(
        hidden_half, in_all, (((1,), (1,)), ((), ())), preferred_element_type=wide
    )
    partial_out = branch_attn + jnp.dot(act_half, down_all, preferred_element_type=wide)
    branch = group.reduce_sequences(partial_out.reshape(seqs, length, D), sent)
    output = (tokens.astype(wide) + branch + (bias_out + bias_down)).astype(half)

    partial_slope = partial_attn * gain_one + partial_mlp * gain_two
    own = batch * length
    own_unit = unit[:own]
    own_cot = cotangent.reshape(own, D).astype(wide)
    slope = group.reduce_sequences(partial_slope.reshape(seqs, length, D), sent)
    slope = slope.reshape(own, D)
    down_marks = []
    down_total = group.from_replicas(
        group.scatter(grad_down.reshape(groups, units, D), 1, down_marks).astype(half)
    )
    scale = lax.rsqrt(spread[:own] + norm_eps)
    back = scale * (
        slope
        - jnp.mean(slope, axis=-1, keepdims=True)
        - own_unit * jnp.mean(slope * own_unit, axis=-1, keepdims=True)
    )
    input_grad = (own_cot + back).reshape(batch, length, D)

    def columns(values, outer):
        zero = jnp.zeros((outer, ways, values.shape[0] // outer), wide)
        return lax.dynamic_update_slice(
            zero, values.reshape(outer, 1, -1), (0, group.rank, 0)
        ).reshape(-1)

    column_sum = jnp.sum(own_cot, axis=0)
    vector_grad = jnp.concatenate(
        [
            jnp.sum(partial_attn * unit, axis=0),
            jnp.sum(partial_attn, axis=0),
            jnp.sum(partial_mlp * unit, axis=0),
            jnp.sum(partial_mlp, axis=0),
            columns(bias_qkv_grad, 3),
            column_sum,
            columns(jnp.sum(grad_hidden, axis=0), groups),
            column_sum,
        ]
    ).reshape(groups, twins, vec_size)
    vector_grad = jnp.pad(
        vector_grad.astype(half), ((0, 0), (0, 0), (0, vec_rows * width - vec_size))
    ).reshape(groups, twins, vec_rows, width)
    in_grad = jnp.concatenate([grad_in.reshape(groups, twins, rows, width), vector_grad], axis=2)
    in_marks = []
    in_total = group.unshare(group.scatter(in_grad, 2, in_marks, sent))
    first_sum = after(first_sum, *in_marks)
    first_total = group.unshare(first_sum[:, : 3 * out_cols].reshape(twins, rows, -1))
    out_sum = first_sum[:, 3 * out_cols :].astype(half).reshape(ways, out_rows, out_cols)
    out_sum = out_sum.transpose(1, 0, 2).reshape(out_rows, D)
    out_total = group.from_replicas(group.to_holders(out_sum)).reshape(rows, D)
    vec_total = jnp.sum(in_total[:, rows:].astype(wide), axis=0).reshape(-1)[:vec_size]

    totals = (
        first_total.reshape(ways, rows, 3, out_cols)
        .transpose(1, 2, 0, 3)
        .reshape(rows, -1)
        .astype(wide),
        out_total.astype(wide),
        in_total[:, :rows]
        .reshape(ways, rows, groups, units)
        .transpose(1, 2, 0, 3)
        .reshape(rows, -1)
        .astype(wide),
        down_total.reshape(-1, D).astype(wide),
        vec_total,
    )
    masters = (w_qkv, w_out, w_in, w_down, vectors)
    firsts = (m_qkv, m_out, m_in, m_down, m_vec)
    seconds = (v_qkv, v_out, v_in, v_down, v_vec)
    decays = (decay_rate, decay_rate, decay_rate, decay_rate, 0.0)
    results = [
        adamw(masters[number], totals[number], firsts[number], seconds[number], decays[number])
        for number in range(5)
    ]
    return (
        output,
        input_grad,
        *totals,
        *(result[0] for result in results),
        *(result[1] for result in results),
        *(result[2] for result in results),
    )


def solution(mesh):
    placed = (
        P(("shard", "replica"), None, None),
        P(("shard", "replica"), None),
        P(("shard", "replica"), None, None),
        P("shard", None),
        P("shard", None),
        P("shard", None),
        P("shard", None),
        P("shard"),
        P("shard", None),
        P("shard", None),
        P("shard", None),
        P("shard", None),
        P("shard"),
        P("shard", None),
        P("shard", None),
        P("shard", None),
        P("shard", None),
        P("shard"),
    )
    return jax.shard_map(
        functools.partial(step, Group(mesh)),
        mesh=mesh,
        in_specs=placed,
        out_specs=(
            P(("shard", "replica"), None, None),
            P(("shard", "replica"), None, None),
            P("shard", None),
            P("shard", None),
            P("shard", None),
            P("shard", None),
            P("shard"),
            P("shard", None),
            P("shard", None),
            P("shard", None),
            P("shard", None),
            P("shard"),
            P("shard", None),
            P("shard", None),
            P("shard", None),
            P("shard", None),
            P("shard"),
            P("shard", None),
            P("shard", None),
            P("shard", None),
            P("shard", None),
            P("shard"),
        ),
        check_vma=False,
    )
```

```python
import functools

import jax
import jax.numpy as jnp
import numpy as np
from jax import lax
from jax.experimental import pallas as pl
from jax.experimental.pallas import tpu as pltpu
from jax.sharding import PartitionSpec as P

D = 768
HEADS = 12
HEAD_DIM = 64
FF = 3072
ROT = 16
STEP = 5


norm_eps = 1e-05
learn_rate = 0.01
beta_first = 0.9
beta_second = 0.999
adam_eps = 1e-08
decay_rate = 0.1


def split_vectors(vectors):
    bounds = [0, D, 2 * D, 3 * D, 4 * D, 7 * D, 8 * D, 8 * D + FF, 9 * D + FF]
    return [vectors[bounds[number] : bounds[number + 1]] for number in range(8)]


def rotary_lanes(length, heads):
    half_rot = ROT // 2
    freqs = 10000.0 ** (-np.arange(half_rot) * 2.0 / ROT)
    angles = np.arange(length)[:, None] * freqs[None, :]
    cosine = np.ones((length, HEAD_DIM))
    sine = np.zeros((length, HEAD_DIM))
    cosine[:, :ROT] = np.tile(np.cos(angles), (1, 2))
    sine[:, :ROT] = np.tile(np.sin(angles), (1, 2))
    partner = np.zeros((HEAD_DIM, HEAD_DIM))
    for lane in range(half_rot):
        partner[lane + half_rot, lane] = -1.0
        partner[lane, lane + half_rot] = 1.0
    cosine = jnp.tile(jnp.asarray(cosine, jnp.float32), (1, heads))
    sine = jnp.tile(jnp.asarray(sine, jnp.float32), (1, heads))
    return cosine, sine, jnp.asarray(np.kron(np.eye(heads), partner), jnp.bfloat16)


def contract(left, right, left_dim, right_dim):
    return lax.dot_general(
        left, right, (((left_dim,), (right_dim,)), ((), ())), preferred_element_type=jnp.float32
    )


def attention_kernel(
    ways,
    heads,
    normed_ref,
    cot_ref,
    seg_col_ref,
    seg_row_ref,
    qkv_ref,
    out_ref,
    bias_ref,
    cos_ref,
    sin_ref,
    partner_ref,
    mixed_ref,
    branch_ref,
    slope_ref,
    sums_ref,
    grad_qkv_ref,
    grad_out_ref,
    qkv_total,
    out_total,
):
    half = jnp.bfloat16
    wide = jnp.float32
    step = pl.program_id(0)
    cols = heads * HEAD_DIM
    partner = partner_ref[...]
    cosine = jnp.tile(cos_ref[...], (seg_row_ref.shape[0], 1))
    sine = jnp.tile(sin_ref[...], (seg_row_ref.shape[0], 1))

    def partners(values):
        high = values.astype(half)
        low = (values - high.astype(wide)).astype(half)
        return contract(high, partner, 1, 0) + contract(low, partner, 1, 0)

    normed = normed_ref[...]
    cot = cot_ref[...]
    projected = contract(normed, qkv_ref[...], 1, 0) + bias_ref[...]
    query, keyed = projected[:, :cols], projected[:, cols : 2 * cols]
    query = ((query * cosine + partners(query) * sine) * HEAD_DIM ** (-0.5)).astype(half)
    keyed = (keyed * cosine + partners(keyed) * sine).astype(half)
    valued = projected[:, 2 * cols : 3 * cols].astype(half)
    grad_mixed = contract(cot, out_ref[...], 1, 1).astype(half)
    per_step, length = seg_row_ref.shape[0], seg_row_ref.shape[2]
    row = lax.broadcasted_iota(jnp.int32, (length, length), 0)
    column = lax.broadcasted_iota(jnp.int32, (length, length), 1)
    causal = row >= column
    masks = [(seg_col_ref[seq] == seg_row_ref[seq]) & causal for seq in range(per_step)]
    allowed = [masks[seq] for seq in range(per_step) for _ in range(heads)]

    def parts(values):
        return [
            values[seq * length : (seq + 1) * length, head * HEAD_DIM : (head + 1) * HEAD_DIM]
            for seq in range(per_step)
            for head in range(heads)
        ]

    def whole(values):
        joined = [
            jnp.concatenate(values[seq * heads : (seq + 1) * heads], axis=1)
            for seq in range(per_step)
        ]
        return jnp.concatenate(joined, axis=0) if per_step > 1 else joined[0]

    query, keyed, valued, turned = parts(query), parts(keyed), parts(valued), parts(grad_mixed)
    scores = [
        jnp.where(mask, contract(q, k, 1, 1), -1e30) for mask, q, k in zip(allowed, query, keyed)
    ]
    grad_probs = [contract(g, v, 1, 1) for g, v in zip(turned, valued)]
    shifted = [jnp.exp(score - jnp.max(score, axis=1, keepdims=True)) for score in scores]
    probs_full = [part * (1.0 / jnp.sum(part, axis=1, keepdims=True)) for part in shifted]
    probs = [part.astype(half) for part in probs_full]
    mixed = [contract(part, v, 1, 0) for part, v in zip(probs, valued)]
    inner = [
        jnp.sum(blend * g.astype(wide), axis=1, keepdims=True) for blend, g in zip(mixed, turned)
    ]
    grad_scores = [
        (part * (grad - shift)).astype(half)
        for part, grad, shift in zip(probs_full, grad_probs, inner)
    ]
    grad_v = [contract(part, g, 0, 0) for part, g in zip(probs, turned)]
    grad_q = [contract(part, k, 1, 0) * HEAD_DIM ** (-0.5) for part, k in zip(grad_scores, keyed)]
    grad_k = [contract(part, q, 0, 0) for part, q in zip(grad_scores, query)]
    mixed = whole(mixed).astype(half)
    grad_q, grad_k, grad_v = whole(grad_q), whole(grad_k), whole(grad_v)
    grad_q = grad_q * cosine - partners(grad_q) * sine
    grad_k = grad_k * cosine - partners(grad_k) * sine
    grad_projected = jnp.concatenate([grad_q, grad_k, grad_v, jnp.zeros_like(grad_v)], axis=1)
    projected_half = grad_projected.astype(half)
    sums_ref[0] = jnp.sum(grad_projected, axis=0, keepdims=True)
    mixed_ref[...] = mixed
    branch_ref[...] = contract(mixed, out_ref[...], 1, 0)
    slope_ref[...] = contract(projected_half, qkv_ref[...], 1, 1)

    @pl.when(step == 0)
    def _():
        qkv_total[...] = jnp.zeros_like(qkv_total)
        out_total[...] = jnp.zeros_like(out_total)

    qkv_total[...] += contract(normed, projected_half, 0, 0)
    out_total[...] += contract(mixed, cot, 0, 0)

    @pl.when(step == pl.num_programs(0) - 1)
    def _():
        grad_qkv_ref[...] = qkv_total[...].astype(half)
        for way in range(ways):
            grad_out_ref[way] = out_total[:, way * cols : (way + 1) * cols].astype(half)


def attention(normed, cot, seg, qkv_all, out_all, bias, ways, heads):
    half = jnp.bfloat16
    wide = jnp.float32
    seqs, length = seg.shape
    count = seqs * length
    cols = heads * HEAD_DIM
    width = qkv_all.shape[1]
    per_step = 4 if seqs % 4 == 0 else 1
    block_rows = per_step * length
    cosine, sine, partner = rotary_lanes(length, heads)
    bias_row = jnp.pad(bias, (0, width - 3 * cols))[None]

    def block(rows, lanes):
        return pl.BlockSpec((rows, lanes), lambda s: (s, 0))

    def whole(*shape):
        return pl.BlockSpec(shape, lambda s: (0,) * len(shape))

    flops = 2 * count * (2 * D * width * 2 + 3 * D * cols + 7 * length * cols)
    return pl.pallas_call(
        functools.partial(attention_kernel, ways, heads),
        grid=(seqs // per_step,),
        in_specs=[
            block(block_rows, D),
            block(block_rows, D),
            pl.BlockSpec((per_step, length, 1), lambda s: (s, 0, 0)),
            pl.BlockSpec((per_step, 1, length), lambda s: (s, 0, 0)),
            whole(D, width),
            whole(cols, D),
            whole(1, width),
            whole(length, cols),
            whole(length, cols),
            whole(cols, cols),
        ],
        out_specs=[
            block(block_rows, cols),
            block(block_rows, D),
            block(block_rows, D),
            pl.BlockSpec((1, 1, width), lambda s: (s, 0, 0)),
            whole(D, width),
            whole(ways, cols, cols),
        ],
        out_shape=[
            jax.ShapeDtypeStruct((count, cols), half),
            jax.ShapeDtypeStruct((count, D), wide),
            jax.ShapeDtypeStruct((count, D), wide),
            jax.ShapeDtypeStruct((seqs // per_step, 1, width), wide),
            jax.ShapeDtypeStruct((D, width), half),
            jax.ShapeDtypeStruct((ways, cols, cols), half),
        ],
        scratch_shapes=[pltpu.VMEM((D, width), wide), pltpu.VMEM((cols, D), wide)],
        compiler_params=pltpu.CompilerParams(dimension_semantics=("arbitrary",)),
        cost_estimate=pl.CostEstimate(
            flops=flops, bytes_accessed=18 * 1024 * 1024, transcendentals=seqs * heads * length**2
        ),
        name="attention_block",
    )(
        normed,
        cot,
        seg[:, :, None],
        seg[:, None, :],
        qkv_all,
        out_all,
        bias_row,
        cosine,
        sine,
        partner,
    )


class Group:
    def __init__(self, mesh):
        self.shards = mesh.shape["shard"]
        self.replicas = mesh.shape["replica"]
        self.rings = self.shards <= 16 and self.shards % 4 == 0
        self.twins = 2 if self.rings and HEADS % (2 * self.replicas) == 0 else 1
        self.ways = self.twins * self.replicas
        self.groups = self.shards // self.twins
        self.pairs = 2 if self.groups % 2 == 0 else 1
        self.lines = self.groups // self.pairs

    def place(self):
        shard = lax.axis_index("shard")
        self.twin = shard % self.twins
        self.group = shard // self.twins
        self.pair = self.group % self.pairs
        self.line = self.group // self.pairs
        self.replica = lax.axis_index("replica")
        self.rank = self.twin * self.replicas + self.replica


    def from_twin(self, array):
        return lax.ppermute(array, "shard", [(s, s ^ 1) for s in range(self.shards)])

    def from_pair(self, array):
        step = self.twins
        return lax.ppermute(array, "shard", [(s, s ^ step) for s in range(self.shards)])

    def along_line(self, array, hops):
        block = self.twins * self.pairs
        return lax.ppermute(
            array,
            "shard",
            [
                (s, ((s // block + hops) % self.lines) * block + s % block)
                for s in range(self.shards)
            ],
        )

    def to_replica(self, array, hops):
        size = self.replicas
        return lax.ppermute(array, "replica", [(c, (c + hops) % size) for c in range(size)])

    def twins_in_order(self, own, far):
        return jnp.stack(
            [jnp.where(self.twin == 0, own, far), jnp.where(self.twin == 0, far, own)]
        )

    def to_rank(self, array, twin_flip, hops):
        size = self.replicas
        pairs = [
            (s * size + c, (s ^ twin_flip) * size + (c + hops) % size)
            for s in range(self.shards)
            for c in range(size)
        ]
        return lax.ppermute(array, ("shard", "replica"), pairs)


    def gather_whole(self, piece):
        members = None
        if self.twins > 1:
            members = [
                [group * self.twins + twin for group in range(self.groups)]
                for twin in range(self.twins)
            ]
        return lax.all_gather(piece, "shard", axis=0, tiled=False, axis_index_groups=members)

    def gather(self, piece):
        if not self.rings:
            return self.gather_whole(piece)
        held = [piece]
        for hops in range(1, self.lines):
            held.append(self.along_line(piece, hops))
        buffer = jnp.zeros((self.groups,) + piece.shape, piece.dtype)
        zeros = (0,) * piece.ndim
        for hops, block in enumerate(held):
            line = (self.line - hops) % self.lines
            own = line * self.pairs + self.pair
            buffer = lax.dynamic_update_slice(buffer, block[None], (own,) + zeros)
        for hops, block in enumerate(held):
            line = (self.line - hops) % self.lines
            other = line * self.pairs + (self.pair ^ 1)
            buffer = lax.dynamic_update_slice(
                buffer, self.from_pair(block)[None], (other,) + zeros
            )
        return buffer

    def scatter(self, terms, pieces=1, marks=None, before=()):
        wide = jnp.float32
        if not self.rings:
            total = lax.psum_scatter(terms.astype(wide), "shard", scatter_dimension=0, tiled=False)
            return total
        halves = terms.reshape((self.lines, self.pairs) + terms.shape[1:])
        keep = lax.dynamic_index_in_dim(halves, self.pair, 1, keepdims=False)
        give = lax.dynamic_index_in_dim(halves, self.pair ^ 1, 1, keepdims=False)

        def block(array, hops):
            return lax.dynamic_index_in_dim(
                array, (self.line + hops) % self.lines, 0, keepdims=False
            )

        order = [hops for hops in range(1, self.lines)] + [0]
        if pieces == 1:
            far = self.from_pair(give)
            merged = keep.astype(wide) + far.astype(wide)
            if before:
                merged = after(merged, *before)
            if marks is not None:
                marks.append(merged)
            sums = {hops: block(merged, hops) for hops in order}
        else:
            sums = {}
            size = -(-self.lines // pieces)
            for start in range(0, self.lines, size):
                chosen = order[start : start + size]
                far = jnp.stack([block(give, hops) for hops in chosen])
                far = self.from_pair(far)
                if before:
                    far = after(far, *before)
                if marks is not None:
                    marks.append(far)
                for place, hops in enumerate(chosen):
                    term = block(keep, hops).astype(wide) + far[place].astype(wide)
                    sums[hops] = term.astype(jnp.bfloat16) if hops else term
        total = sums[0]
        for hops in range(1, self.lines):
            give = sums[hops].astype(jnp.bfloat16)
            far = self.along_line(give, hops)
            total = total + far.astype(wide)
        return total

    def gather_sequences(self, array):
        across = array[None]
        if self.twins == 2:
            across = jnp.stack([array, self.from_twin(array)])
        slots = [across]
        for hops in range(1, self.replicas):
            slots.append(self.to_replica(across, self.replicas - hops))
        return jnp.stack(slots).reshape((-1,) + array.shape[1:])

    def reduce_sequences(self, partial, marks=None):
        wire = jnp.bfloat16
        wide = jnp.float32
        shape = partial.shape
        batch = shape[0] // self.ways
        slots = partial.reshape((self.replicas, self.twins, batch) + shape[1:])
        total = slots[0]
        for hops in range(1, self.replicas):
            far = self.to_replica(slots[hops].astype(wire), hops)
            total = total + far.astype(wide)
        own = total[0]
        if self.twins == 2:
            give = total[1].astype(wire)
            if marks is not None:
                marks.append(give)
            far = self.from_twin(give)
            own = own + far.astype(wide)
        return own


    def share(self, pick):
        own = pick(self.rank)
        if self.twins == 1:
            return own[None]
        far = self.from_twin(pick((self.twin ^ 1) * self.replicas + self.replica))
        return self.twins_in_order(own, far)

    def from_replicas(self, own):
        held = [own] + [self.to_replica(own, hops) for hops in range(1, self.replicas)]
        if self.replicas == 2:
            return jnp.stack(
                [
                    jnp.where(self.replica == 0, held[0], held[1]),
                    jnp.where(self.replica == 0, held[1], held[0]),
                ]
            )
        result = jnp.zeros((self.replicas,) + own.shape, own.dtype)
        for hops, part in enumerate(held):
            source = (self.replica - hops) % self.replicas
            result = lax.dynamic_update_slice(result, part[None], (source,) + (0,) * own.ndim)
        return result

    def unshare(self, rows):
        half = jnp.bfloat16
        own = lax.dynamic_index_in_dim(rows, self.twin, 0, keepdims=False).astype(half)
        if self.twins == 2:
            give = lax.dynamic_index_in_dim(rows, self.twin ^ 1, 0, keepdims=False)
            both = self.twins_in_order(own, self.from_twin(give.astype(half)))
        else:
            both = own[None]
        stacked = jnp.swapaxes(self.from_replicas(both), 0, 1)
        return stacked.reshape((self.ways,) + own.shape)

    def routes(self):
        pairs = []
        for holder in range(self.shards * self.replicas):
            rank, group = holder // self.groups, holder % self.groups
            shard = group * self.twins + rank // self.replicas
            pairs.append((holder, shard * self.replicas + rank % self.replicas))
        return pairs

    def to_users(self, piece):
        return lax.ppermute(piece, ("shard", "replica"), self.routes())

    def to_holders(self, piece):
        back = [(user, holder) for holder, user in self.routes()]
        return lax.ppermute(piece, ("shard", "replica"), back)


def after(value, *earlier):
    return lax.optimization_barrier((value, *earlier))[0]


def adamw(weight, gradient, moment_one, moment_two, decay_on):
    moment_one = beta_first * moment_one + (1.0 - beta_first) * gradient
    moment_two = beta_second * moment_two + (1.0 - beta_second) * gradient * gradient
    first_hat = moment_one / (1.0 - beta_first**STEP)
    second_hat = moment_two / (1.0 - beta_second**STEP)
    updated = weight - learn_rate * (
        first_hat / (jnp.sqrt(second_hat) + adam_eps) + decay_on * weight
    )
    return (updated, moment_one, moment_two)


def step(
    group,
    tokens,
    segment_ids,
    cotangent,
    w_qkv,
    w_out,
    w_in,
    w_down,
    vectors,
    m_qkv,
    m_out,
    m_in,
    m_down,
    m_vec,
    v_qkv,
    v_out,
    v_in,
    v_down,
    v_vec,
):
    group.place()
    half = jnp.bfloat16
    wide = jnp.float32
    ways = group.ways
    groups = group.groups
    twins = group.twins
    heads = HEADS // ways
    rows = w_qkv.shape[0]
    units = FF // (groups * ways)
    out_cols = D // ways
    width = 4 * out_cols
    batch, length = tokens.shape[:2]
    seqs = batch * ways
    count = seqs * length
    vec_size = vectors.shape[0]
    vec_rows = -(-vec_size // (8 * width)) * 8

    qkv_half = w_qkv.astype(half).reshape(rows, 3, ways, out_cols)
    in_half = w_in.astype(half).reshape(rows, groups, ways, units)
    down_half = w_down.astype(half).reshape(group.replicas, units, D)
    vec_half = jnp.pad(vectors.astype(half), (0, vec_rows * width - vec_size))
    vec_half = vec_half.reshape(vec_rows, width)
    out_rows = rows // group.replicas
    out_half = lax.dynamic_slice_in_dim(w_out, group.replica * out_rows, out_rows, 0)
    out_piece = group.to_users(out_half.astype(half))
    out_piece = out_piece.reshape(out_rows, ways, out_cols).transpose(1, 0, 2)

    def pick(rank):
        qkv = lax.dynamic_index_in_dim(qkv_half, rank, 2, keepdims=False).reshape(rows, -1)
        qkv = jnp.concatenate([qkv, jnp.zeros((rows, out_cols), half)], axis=1)
        into = lax.dynamic_index_in_dim(in_half, rank, 2, keepdims=False).reshape(rows, -1)
        return jnp.concatenate([qkv, vec_half, into], axis=0)

    shared = group.share(pick)
    down_piece = lax.dynamic_index_in_dim(down_half, group.replica, 0, keepdims=False)
    second_piece = jnp.concatenate(
        [shared[:, rows + vec_rows :].reshape(-1, width), down_piece.reshape(-1, width)], axis=0
    )
    second = group.gather_whole(second_piece)
    first_piece = lax.dynamic_update_slice(
        shared[:, : rows + vec_rows],
        out_piece.reshape(twins, rows, out_cols),
        (0, 0, 3 * out_cols),
    )

    seg_rows = jnp.pad(segment_ids.astype(half)[:, None], ((0, 0), (0, 7), (0, D - length)))
    pack = jnp.concatenate([tokens, cotangent, seg_rows], axis=1)
    packs = group.gather_sequences(after(pack, shared))
    x_seqs = packs[:, :length]
    cot = packs[:, length : 2 * length]
    seg = packs[:, 2 * length, :length].astype(wide)

    first = group.gather(first_piece)
    qkv_all = first[:, :, :rows].reshape(D, width)
    vec_all = first[:, :, rows:].reshape(group.shards, -1)[:, :vec_size].reshape(-1).astype(wide)
    in_all = second[:, : twins * rows].reshape(D, width)
    down_all = second[:, twins * rows :].reshape(width, D)
    out_all = first[:, :, :rows, 3 * out_cols :].reshape(groups, ways, out_rows, out_cols)
    out_all = out_all.transpose(0, 2, 1, 3).reshape(out_cols, D)

    gain_one, offset_one, gain_two, offset_two, bias_qkv, bias_out, bias_in, bias_down = (
        split_vectors(vec_all)
    )
    bias_qkv_own = lax.dynamic_index_in_dim(
        bias_qkv.reshape(3, ways, -1), group.rank, 1, keepdims=False
    ).reshape(-1)
    bias_in_own = lax.dynamic_index_in_dim(
        bias_in.reshape(groups, ways, units), group.rank, 1, keepdims=False
    ).reshape(-1)

    inputs = x_seqs.reshape(count, D).astype(wide)
    center = inputs - jnp.mean(inputs, axis=-1, keepdims=True)
    spread = jnp.mean(center * center, axis=-1, keepdims=True)
    unit = center * lax.rsqrt(spread + norm_eps)
    normed_attn = (unit * gain_one + offset_one).astype(half)
    normed_mlp = (unit * gain_two + offset_two).astype(half)
    cot_flat = cot.reshape(count, D)
    _, branch_attn, partial_attn, sums_attn, grad_qkv, grad_out = attention(
        normed_attn, cot_flat, seg, qkv_all, out_all, bias_qkv_own, ways, heads
    )
    bias_qkv_grad = jnp.sum(sums_attn, axis=(0, 1))[: 3 * out_cols]
    out_back = grad_out.reshape(ways, groups, out_rows, out_cols).transpose(1, 0, 2, 3)
    first_grad = jnp.concatenate(
        [
            grad_qkv[:, : 3 * out_cols].reshape(groups, twins * rows, -1),
            out_back.reshape(groups, twins * rows, out_cols),
        ],
        axis=2,
    )
    marks = []
    first_sum = group.scatter(first_grad, 1, marks)
    hidden = jnp.dot(normed_mlp, in_all, preferred_element_type=wide) + bias_in_own
    share_below = 0.5 + 0.5 * lax.erf(hidden * 0.5**0.5)
    act_half = (hidden * share_below).astype(half)
    grad_down = lax.dot_general(
        act_half, cot_flat, (((0,), (0,)), ((), ())), preferred_element_type=wide
    ).astype(half)
    sent = []
    back_cot = after(cot_flat, grad_down, *marks)
    grad_act = contract(back_cot, down_all, 1, 1)
    density = jnp.exp(-0.5 * hidden * hidden) * (2.0 * np.pi) ** -0.5
    grad_hidden = grad_act * (share_below + hidden * density)
    hidden_half = grad_hidden.astype(half)
    grad_in = lax.dot_general(
        normed_mlp, hidden_half, (((0,), (0,)), ((), ())), preferred_element_type=wide
    ).astype(half)
    partial_mlp = lax.dot_general(
        hidden_half, in_all, (((1,), (1,)), ((), ())), preferred_element_type=wide
    )
    partial_out = branch_attn + jnp.dot(act_half, down_all, preferred_element_type=wide)
    branch = group.reduce_sequences(partial_out.reshape(seqs, length, D), sent)
    output = (tokens.astype(wide) + branch + (bias_out + bias_down)).astype(half)

    partial_slope = partial_attn * gain_one + partial_mlp * gain_two
    own = batch * length
    own_unit = unit[:own]
    own_cot = cotangent.reshape(own, D).astype(wide)
    slope = group.reduce_sequences(partial_slope.reshape(seqs, length, D), sent)
    slope = slope.reshape(own, D)
    down_marks = []
    down_total = group.from_replicas(
        group.scatter(grad_down.reshape(groups, units, D), 1, down_marks).astype(half)
    )
    scale = lax.rsqrt(spread[:own] + norm_eps)
    back = scale * (
        slope
        - jnp.mean(slope, axis=-1, keepdims=True)
        - own_unit * jnp.mean(slope * own_unit, axis=-1, keepdims=True)
    )
    input_grad = (own_cot + back).reshape(batch, length, D)

    def columns(values, outer):
        zero = jnp.zeros((outer, ways, values.shape[0] // outer), wide)
        return lax.dynamic_update_slice(
            zero, values.reshape(outer, 1, -1), (0, group.rank, 0)
        ).reshape(-1)

    column_sum = jnp.sum(own_cot, axis=0)
    vector_grad = jnp.concatenate(
        [
            jnp.sum(partial_attn * unit, axis=0),
            jnp.sum(partial_attn, axis=0),
            jnp.sum(partial_mlp * unit, axis=0),
            jnp.sum(partial_mlp, axis=0),
            columns(bias_qkv_grad, 3),
            column_sum,
            columns(jnp.sum(grad_hidden, axis=0), groups),
            column_sum,
        ]
    ).reshape(groups, twins, vec_size)
    vector_grad = jnp.pad(
        vector_grad.astype(half), ((0, 0), (0, 0), (0, vec_rows * width - vec_size))
    ).reshape(groups, twins, vec_rows, width)
    in_grad = jnp.concatenate([grad_in.reshape(groups, twins, rows, width), vector_grad], axis=2)
    in_marks = []
    in_total = group.unshare(group.scatter(in_grad, 2, in_marks, sent))
    first_sum = after(first_sum, *in_marks)
    first_total = group.unshare(first_sum[:, : 3 * out_cols].reshape(twins, rows, -1))
    out_sum = first_sum[:, 3 * out_cols :].astype(half).reshape(ways, out_rows, out_cols)
    out_sum = out_sum.transpose(1, 0, 2).reshape(out_rows, D)
    out_total = group.from_replicas(group.to_holders(out_sum)).reshape(rows, D)
    vec_total = jnp.sum(in_total[:, rows:].astype(wide), axis=0).reshape(-1)[:vec_size]

    totals = (
        first_total.reshape(ways, rows, 3, out_cols)
        .transpose(1, 2, 0, 3)
        .reshape(rows, -1)
        .astype(wide),
        out_total.astype(wide),
        in_total[:, :rows]
        .reshape(ways, rows, groups, units)
        .transpose(1, 2, 0, 3)
        .reshape(rows, -1)
        .astype(wide),
        down_total.reshape(-1, D).astype(wide),
        vec_total,
    )
    masters = (w_qkv, w_out, w_in, w_down, vectors)
    firsts = (m_qkv, m_out, m_in, m_down, m_vec)
    seconds = (v_qkv, v_out, v_in, v_down, v_vec)
    decays = (decay_rate, decay_rate, decay_rate, decay_rate, 0.0)
    results = [
        adamw(masters[number], totals[number], firsts[number], seconds[number], decays[number])
        for number in range(5)
    ]
    return (
        output,
        input_grad,
        *totals,
        *(result[0] for result in results),
        *(result[1] for result in results),
        *(result[2] for result in results),
    )


def solution(mesh):
    placed = (
        P(("shard", "replica"), None, None),
        P(("shard", "replica"), None),
        P(("shard", "replica"), None, None),
        P("shard", None),
        P("shard", None),
        P("shard", None),
        P("shard", None),
        P("shard"),
        P("shard", None),
        P("shard", None),
        P("shard", None),
        P("shard", None),
        P("shard"),
        P("shard", None),
        P("shard", None),
        P("shard", None),
        P("shard", None),
        P("shard"),
    )
    return jax.shard_map(
        functools.partial(step, Group(mesh)),
        mesh=mesh,
        in_specs=placed,
        out_specs=(
            P(("shard", "replica"), None, None),
            P(("shard", "replica"), None, None),
            P("shard", None),
            P("shard", None),
            P("shard", None),
            P("shard", None),
            P("shard"),
            P("shard", None),
            P("shard", None),
            P("shard", None),
            P("shard", None),
            P("shard"),
            P("shard", None),
            P("shard", None),
            P("shard", None),
            P("shard", None),
            P("shard"),
            P("shard", None),
            P("shard", None),
            P("shard", None),
            P("shard", None),
            P("shard"),
        ),
        check_vma=False,
    )
```

```python
import functools

import jax
import jax.numpy as jnp
import numpy as np
from jax import lax
from jax.experimental import pallas as pl
from jax.experimental.pallas import tpu as pltpu
from jax.sharding import PartitionSpec as P

D = 768
HEADS = 12
HEAD_DIM = 64
FF = 3072
ROT = 16
STEP = 5


norm_eps = 1e-05
learn_rate = 0.01
beta_first = 0.9
beta_second = 0.999
adam_eps = 1e-08
decay_rate = 0.1


def split_vectors(vectors):
    bounds = [0, D, 2 * D, 3 * D, 4 * D, 7 * D, 8 * D, 8 * D + FF, 9 * D + FF]
    return [vectors[bounds[number] : bounds[number + 1]] for number in range(8)]


def rotary_lanes(length, heads):
    half_rot = ROT // 2
    freqs = 10000.0 ** (-np.arange(half_rot) * 2.0 / ROT)
    angles = np.arange(length)[:, None] * freqs[None, :]
    cosine = np.ones((length, HEAD_DIM))
    sine = np.zeros((length, HEAD_DIM))
    cosine[:, :ROT] = np.tile(np.cos(angles), (1, 2))
    sine[:, :ROT] = np.tile(np.sin(angles), (1, 2))
    partner = np.zeros((HEAD_DIM, HEAD_DIM))
    for lane in range(half_rot):
        partner[lane + half_rot, lane] = -1.0
        partner[lane, lane + half_rot] = 1.0
    cosine = jnp.tile(jnp.asarray(cosine, jnp.float32), (1, heads))
    sine = jnp.tile(jnp.asarray(sine, jnp.float32), (1, heads))
    return cosine, sine, jnp.asarray(np.kron(np.eye(heads), partner), jnp.bfloat16)


def contract(left, right, left_dim, right_dim):
    return lax.dot_general(
        left, right, (((left_dim,), (right_dim,)), ((), ())), preferred_element_type=jnp.float32
    )


def attention_kernel(
    ways,
    heads,
    normed_ref,
    cot_ref,
    seg_col_ref,
    seg_row_ref,
    qkv_ref,
    out_ref,
    bias_ref,
    cos_ref,
    sin_ref,
    partner_ref,
    mixed_ref,
    grad_ref,
    sums_ref,
    grad_qkv_ref,
    grad_out_ref,
    qkv_total,
    out_total,
):
    half = jnp.bfloat16
    wide = jnp.float32
    step = pl.program_id(0)
    cols = heads * HEAD_DIM
    partner = partner_ref[...]
    cosine = jnp.tile(cos_ref[...], (seg_row_ref.shape[0], 1))
    sine = jnp.tile(sin_ref[...], (seg_row_ref.shape[0], 1))

    def partners(values):
        high = values.astype(half)
        low = (values - high.astype(wide)).astype(half)
        return contract(high, partner, 1, 0) + contract(low, partner, 1, 0)

    normed = normed_ref[...]
    cot = cot_ref[...]
    projected = contract(normed, qkv_ref[...], 1, 0) + bias_ref[...]
    query, keyed = projected[:, :cols], projected[:, cols : 2 * cols]
    query = ((query * cosine + partners(query) * sine) * HEAD_DIM ** (-0.5)).astype(half)
    keyed = (keyed * cosine + partners(keyed) * sine).astype(half)
    valued = projected[:, 2 * cols : 3 * cols].astype(half)
    grad_mixed = contract(cot, out_ref[...], 1, 1).astype(half)
    per_step, length = seg_row_ref.shape[0], seg_row_ref.shape[2]
    row = lax.broadcasted_iota(jnp.int32, (length, length), 0)
    column = lax.broadcasted_iota(jnp.int32, (length, length), 1)
    causal = row >= column
    masks = [(seg_col_ref[seq] == seg_row_ref[seq]) & causal for seq in range(per_step)]
    allowed = [masks[seq] for seq in range(per_step) for _ in range(heads)]

    def parts(values):
        return [
            values[seq * length : (seq + 1) * length, head * HEAD_DIM : (head + 1) * HEAD_DIM]
            for seq in range(per_step)
            for head in range(heads)
        ]

    def whole(values):
        joined = [
            jnp.concatenate(values[seq * heads : (seq + 1) * heads], axis=1)
            for seq in range(per_step)
        ]
        return jnp.concatenate(joined, axis=0) if per_step > 1 else joined[0]

    query, keyed, valued, turned = parts(query), parts(keyed), parts(valued), parts(grad_mixed)
    scores = [
        jnp.where(mask, contract(q, k, 1, 1), -1e30) for mask, q, k in zip(allowed, query, keyed)
    ]
    grad_probs = [contract(g, v, 1, 1) for g, v in zip(turned, valued)]
    shifted = [jnp.exp(score - jnp.max(score, axis=1, keepdims=True)) for score in scores]
    probs_full = [part * (1.0 / jnp.sum(part, axis=1, keepdims=True)) for part in shifted]
    probs = [part.astype(half) for part in probs_full]
    mixed = [contract(part, v, 1, 0) for part, v in zip(probs, valued)]
    inner = [
        jnp.sum(blend * g.astype(wide), axis=1, keepdims=True) for blend, g in zip(mixed, turned)
    ]
    grad_scores = [
        (part * (grad - shift)).astype(half)
        for part, grad, shift in zip(probs_full, grad_probs, inner)
    ]
    grad_v = [contract(part, g, 0, 0) for part, g in zip(probs, turned)]
    grad_q = [contract(part, k, 1, 0) * HEAD_DIM ** (-0.5) for part, k in zip(grad_scores, keyed)]
    grad_k = [contract(part, q, 0, 0) for part, q in zip(grad_scores, query)]
    mixed = whole(mixed).astype(half)
    grad_q, grad_k, grad_v = whole(grad_q), whole(grad_k), whole(grad_v)
    grad_q = grad_q * cosine - partners(grad_q) * sine
    grad_k = grad_k * cosine - partners(grad_k) * sine
    grad_projected = jnp.concatenate([grad_q, grad_k, grad_v, jnp.zeros_like(grad_v)], axis=1)
    projected_half = grad_projected.astype(half)
    sums_ref[0] = jnp.sum(grad_projected, axis=0, keepdims=True)
    mixed_ref[...] = mixed
    grad_ref[...] = projected_half

    @pl.when(step == 0)
    def _():
        qkv_total[...] = jnp.zeros_like(qkv_total)
        out_total[...] = jnp.zeros_like(out_total)

    qkv_total[...] += contract(normed, projected_half, 0, 0)
    out_total[...] += contract(mixed, cot, 0, 0)

    @pl.when(step == pl.num_programs(0) - 1)
    def _():
        grad_qkv_ref[...] = qkv_total[...].astype(half)
        for way in range(ways):
            grad_out_ref[way] = out_total[:, way * cols : (way + 1) * cols].astype(half)


def attention(normed, cot, seg, qkv_all, out_all, bias, ways, heads):
    half = jnp.bfloat16
    wide = jnp.float32
    seqs, length = seg.shape
    count = seqs * length
    cols = heads * HEAD_DIM
    width = qkv_all.shape[1]
    per_step = 2 if seqs % 2 == 0 else 1
    block_rows = per_step * length
    cosine, sine, partner = rotary_lanes(length, heads)
    bias_row = jnp.pad(bias, (0, width - 3 * cols))[None]

    def block(rows, lanes):
        return pl.BlockSpec((rows, lanes), lambda s: (s, 0))

    def whole(*shape):
        return pl.BlockSpec(shape, lambda s: (0,) * len(shape))

    flops = 2 * count * (2 * D * width * 2 + 3 * D * cols + 7 * length * cols)
    return pl.pallas_call(
        functools.partial(attention_kernel, ways, heads),
        grid=(seqs // per_step,),
        in_specs=[
            block(block_rows, D),
            block(block_rows, D),
            pl.BlockSpec((per_step, length, 1), lambda s: (s, 0, 0)),
            pl.BlockSpec((per_step, 1, length), lambda s: (s, 0, 0)),
            whole(D, width),
            whole(cols, D),
            whole(1, width),
            whole(length, cols),
            whole(length, cols),
            whole(cols, cols),
        ],
        out_specs=[
            block(block_rows, cols),
            block(block_rows, width),
            pl.BlockSpec((1, 1, width), lambda s: (s, 0, 0)),
            whole(D, width),
            whole(ways, cols, cols),
        ],
        out_shape=[
            jax.ShapeDtypeStruct((count, cols), half),
            jax.ShapeDtypeStruct((count, width), half),
            jax.ShapeDtypeStruct((seqs // per_step, 1, width), wide),
            jax.ShapeDtypeStruct((D, width), half),
            jax.ShapeDtypeStruct((ways, cols, cols), half),
        ],
        scratch_shapes=[pltpu.VMEM((D, width), wide), pltpu.VMEM((cols, D), wide)],
        compiler_params=pltpu.CompilerParams(dimension_semantics=("arbitrary",)),
        cost_estimate=pl.CostEstimate(
            flops=flops, bytes_accessed=18 * 1024 * 1024, transcendentals=seqs * heads * length**2
        ),
        name="attention_block",
    )(
        normed,
        cot,
        seg[:, :, None],
        seg[:, None, :],
        qkv_all,
        out_all,
        bias_row,
        cosine,
        sine,
        partner,
    )


class Group:
    def __init__(self, mesh):
        self.shards = mesh.shape["shard"]
        self.replicas = mesh.shape["replica"]
        self.rings = self.shards <= 16 and self.shards % 4 == 0
        self.twins = 2 if self.rings and HEADS % (2 * self.replicas) == 0 else 1
        self.ways = self.twins * self.replicas
        self.groups = self.shards // self.twins
        self.pairs = 2 if self.groups % 2 == 0 else 1
        self.lines = self.groups // self.pairs

    def place(self):
        shard = lax.axis_index("shard")
        self.twin = shard % self.twins
        self.group = shard // self.twins
        self.pair = self.group % self.pairs
        self.line = self.group // self.pairs
        self.replica = lax.axis_index("replica")
        self.rank = self.twin * self.replicas + self.replica


    def from_twin(self, array):
        return lax.ppermute(array, "shard", [(s, s ^ 1) for s in range(self.shards)])

    def from_pair(self, array):
        step = self.twins
        return lax.ppermute(array, "shard", [(s, s ^ step) for s in range(self.shards)])

    def along_line(self, array, hops):
        block = self.twins * self.pairs
        return lax.ppermute(
            array,
            "shard",
            [
                (s, ((s // block + hops) % self.lines) * block + s % block)
                for s in range(self.shards)
            ],
        )

    def to_replica(self, array, hops):
        size = self.replicas
        return lax.ppermute(array, "replica", [(c, (c + hops) % size) for c in range(size)])

    def twins_in_order(self, own, far):
        return jnp.stack(
            [jnp.where(self.twin == 0, own, far), jnp.where(self.twin == 0, far, own)]
        )

    def to_rank(self, array, twin_flip, hops):
        size = self.replicas
        pairs = [
            (s * size + c, (s ^ twin_flip) * size + (c + hops) % size)
            for s in range(self.shards)
            for c in range(size)
        ]
        return lax.ppermute(array, ("shard", "replica"), pairs)


    def gather_whole(self, piece):
        members = None
        if self.twins > 1:
            members = [
                [group * self.twins + twin for group in range(self.groups)]
                for twin in range(self.twins)
            ]
        return lax.all_gather(piece, "shard", axis=0, tiled=False, axis_index_groups=members)

    def gather(self, piece):
        if not self.rings:
            return self.gather_whole(piece)
        held = [piece]
        for hops in range(1, self.lines):
            held.append(self.along_line(piece, hops))
        buffer = jnp.zeros((self.groups,) + piece.shape, piece.dtype)
        zeros = (0,) * piece.ndim
        for hops, block in enumerate(held):
            line = (self.line - hops) % self.lines
            own = line * self.pairs + self.pair
            buffer = lax.dynamic_update_slice(buffer, block[None], (own,) + zeros)
        for hops, block in enumerate(held):
            line = (self.line - hops) % self.lines
            other = line * self.pairs + (self.pair ^ 1)
            buffer = lax.dynamic_update_slice(
                buffer, self.from_pair(block)[None], (other,) + zeros
            )
        return buffer

    def scatter(self, terms, pieces=1, marks=None, before=()):
        wide = jnp.float32
        if not self.rings:
            total = lax.psum_scatter(terms.astype(wide), "shard", scatter_dimension=0, tiled=False)
            return total
        halves = terms.reshape((self.lines, self.pairs) + terms.shape[1:])
        keep = lax.dynamic_index_in_dim(halves, self.pair, 1, keepdims=False)
        give = lax.dynamic_index_in_dim(halves, self.pair ^ 1, 1, keepdims=False)

        def block(array, hops):
            return lax.dynamic_index_in_dim(
                array, (self.line + hops) % self.lines, 0, keepdims=False
            )

        order = [hops for hops in range(1, self.lines)] + [0]
        if pieces == 1:
            far = self.from_pair(give)
            merged = keep.astype(wide) + far.astype(wide)
            if before:
                merged = after(merged, *before)
            if marks is not None:
                marks.append(merged)
            sums = {hops: block(merged, hops) for hops in order}
        else:
            sums = {}
            size = -(-self.lines // pieces)
            for start in range(0, self.lines, size):
                chosen = order[start : start + size]
                far = jnp.stack([block(give, hops) for hops in chosen])
                far = self.from_pair(far)
                if before:
                    far = after(far, *before)
                if marks is not None:
                    marks.append(far)
                for place, hops in enumerate(chosen):
                    term = block(keep, hops).astype(wide) + far[place].astype(wide)
                    sums[hops] = term.astype(jnp.bfloat16) if hops else term
        total = sums[0]
        for hops in range(1, self.lines):
            give = sums[hops].astype(jnp.bfloat16)
            far = self.along_line(give, hops)
            total = total + far.astype(wide)
        return total

    def gather_sequences(self, array):
        across = array[None]
        if self.twins == 2:
            across = jnp.stack([array, self.from_twin(array)])
        slots = [across]
        for hops in range(1, self.replicas):
            slots.append(self.to_replica(across, self.replicas - hops))
        return jnp.stack(slots).reshape((-1,) + array.shape[1:])

    def reduce_sequences(self, partial, marks=None):
        wire = jnp.bfloat16
        wide = jnp.float32
        shape = partial.shape
        batch = shape[0] // self.ways
        slots = partial.reshape((self.replicas, self.twins, batch) + shape[1:])
        total = slots[0]
        for hops in range(1, self.replicas):
            far = self.to_replica(slots[hops].astype(wire), hops)
            total = total + far.astype(wide)
        own = total[0]
        if self.twins == 2:
            give = total[1].astype(wire)
            if marks is not None:
                marks.append(give)
            far = self.from_twin(give)
            own = own + far.astype(wide)
        return own


    def share(self, pick):
        own = pick(self.rank)
        if self.twins == 1:
            return own[None]
        far = self.from_twin(pick((self.twin ^ 1) * self.replicas + self.replica))
        return self.twins_in_order(own, far)

    def from_replicas(self, own):
        held = [own] + [self.to_replica(own, hops) for hops in range(1, self.replicas)]
        if self.replicas == 2:
            return jnp.stack(
                [
                    jnp.where(self.replica == 0, held[0], held[1]),
                    jnp.where(self.replica == 0, held[1], held[0]),
                ]
            )
        result = jnp.zeros((self.replicas,) + own.shape, own.dtype)
        for hops, part in enumerate(held):
            source = (self.replica - hops) % self.replicas
            result = lax.dynamic_update_slice(result, part[None], (source,) + (0,) * own.ndim)
        return result

    def unshare(self, rows):
        half = jnp.bfloat16
        own = lax.dynamic_index_in_dim(rows, self.twin, 0, keepdims=False).astype(half)
        if self.twins == 2:
            give = lax.dynamic_index_in_dim(rows, self.twin ^ 1, 0, keepdims=False)
            both = self.twins_in_order(own, self.from_twin(give.astype(half)))
        else:
            both = own[None]
        stacked = jnp.swapaxes(self.from_replicas(both), 0, 1)
        return stacked.reshape((self.ways,) + own.shape)

    def routes(self):
        pairs = []
        for holder in range(self.shards * self.replicas):
            rank, group = holder // self.groups, holder % self.groups
            shard = group * self.twins + rank // self.replicas
            pairs.append((holder, shard * self.replicas + rank % self.replicas))
        return pairs

    def to_users(self, piece):
        return lax.ppermute(piece, ("shard", "replica"), self.routes())

    def to_holders(self, piece):
        back = [(user, holder) for holder, user in self.routes()]
        return lax.ppermute(piece, ("shard", "replica"), back)


def after(value, *earlier):
    return lax.optimization_barrier((value, *earlier))[0]


def adamw(weight, gradient, moment_one, moment_two, decay_on):
    moment_one = beta_first * moment_one + (1.0 - beta_first) * gradient
    moment_two = beta_second * moment_two + (1.0 - beta_second) * gradient * gradient
    first_hat = moment_one / (1.0 - beta_first**STEP)
    second_hat = moment_two / (1.0 - beta_second**STEP)
    updated = weight - learn_rate * (
        first_hat / (jnp.sqrt(second_hat) + adam_eps) + decay_on * weight
    )
    return (updated, moment_one, moment_two)


def step(
    group,
    tokens,
    segment_ids,
    cotangent,
    w_qkv,
    w_out,
    w_in,
    w_down,
    vectors,
    m_qkv,
    m_out,
    m_in,
    m_down,
    m_vec,
    v_qkv,
    v_out,
    v_in,
    v_down,
    v_vec,
):
    group.place()
    half = jnp.bfloat16
    wide = jnp.float32
    ways = group.ways
    groups = group.groups
    twins = group.twins
    heads = HEADS // ways
    rows = w_qkv.shape[0]
    units = FF // (groups * ways)
    out_cols = D // ways
    width = 4 * out_cols
    batch, length = tokens.shape[:2]
    seqs = batch * ways
    count = seqs * length
    vec_size = vectors.shape[0]
    vec_rows = -(-vec_size // (8 * width)) * 8

    qkv_half = w_qkv.astype(half).reshape(rows, 3, ways, out_cols)
    in_half = w_in.astype(half).reshape(rows, groups, ways, units)
    down_half = w_down.astype(half).reshape(group.replicas, units, D)
    vec_half = jnp.pad(vectors.astype(half), (0, vec_rows * width - vec_size))
    vec_half = vec_half.reshape(vec_rows, width)
    out_rows = rows // group.replicas
    out_half = lax.dynamic_slice_in_dim(w_out, group.replica * out_rows, out_rows, 0)
    out_piece = group.to_users(out_half.astype(half))
    out_piece = out_piece.reshape(out_rows, ways, out_cols).transpose(1, 0, 2)

    def pick(rank):
        qkv = lax.dynamic_index_in_dim(qkv_half, rank, 2, keepdims=False).reshape(rows, -1)
        qkv = jnp.concatenate([qkv, jnp.zeros((rows, out_cols), half)], axis=1)
        into = lax.dynamic_index_in_dim(in_half, rank, 2, keepdims=False).reshape(rows, -1)
        return jnp.concatenate([qkv, vec_half, into], axis=0)

    shared = group.share(pick)
    down_piece = lax.dynamic_index_in_dim(down_half, group.replica, 0, keepdims=False)
    second_piece = jnp.concatenate(
        [shared[:, rows + vec_rows :].reshape(-1, width), down_piece.reshape(-1, width)], axis=0
    )
    second = group.gather_whole(second_piece)
    first_piece = lax.dynamic_update_slice(
        shared[:, : rows + vec_rows],
        out_piece.reshape(twins, rows, out_cols),
        (0, 0, 3 * out_cols),
    )

    seg_rows = jnp.pad(segment_ids.astype(half)[:, None], ((0, 0), (0, 7), (0, D - length)))
    pack = jnp.concatenate([tokens, cotangent, seg_rows], axis=1)
    packs = group.gather_sequences(after(pack, shared))
    x_seqs = packs[:, :length]
    cot = packs[:, length : 2 * length]
    seg = packs[:, 2 * length, :length].astype(wide)

    first = group.gather(first_piece)
    qkv_all = first[:, :, :rows].reshape(D, width)
    vec_all = first[:, :, rows:].reshape(group.shards, -1)[:, :vec_size].reshape(-1).astype(wide)
    in_all = second[:, : twins * rows].reshape(D, width)
    down_all = second[:, twins * rows :].reshape(width, D)
    out_all = first[:, :, :rows, 3 * out_cols :].reshape(groups, ways, out_rows, out_cols)
    out_all = out_all.transpose(0, 2, 1, 3).reshape(out_cols, D)

    gain_one, offset_one, gain_two, offset_two, bias_qkv, bias_out, bias_in, bias_down = (
        split_vectors(vec_all)
    )
    bias_qkv_own = lax.dynamic_index_in_dim(
        bias_qkv.reshape(3, ways, -1), group.rank, 1, keepdims=False
    ).reshape(-1)
    bias_in_own = lax.dynamic_index_in_dim(
        bias_in.reshape(groups, ways, units), group.rank, 1, keepdims=False
    ).reshape(-1)

    inputs = x_seqs.reshape(count, D).astype(wide)
    center = inputs - jnp.mean(inputs, axis=-1, keepdims=True)
    spread = jnp.mean(center * center, axis=-1, keepdims=True)
    unit = center * lax.rsqrt(spread + norm_eps)
    normed_attn = (unit * gain_one + offset_one).astype(half)
    normed_mlp = (unit * gain_two + offset_two).astype(half)
    cot_flat = cot.reshape(count, D)
    mixed, projected_half, sums_attn, grad_qkv, grad_out = attention(
        normed_attn, cot_flat, seg, qkv_all, out_all, bias_qkv_own, ways, heads
    )
    partial_attn = contract(projected_half, qkv_all, 1, 1)
    bias_qkv_grad = jnp.sum(sums_attn, axis=(0, 1))[: 3 * out_cols]
    out_back = grad_out.reshape(ways, groups, out_rows, out_cols).transpose(1, 0, 2, 3)
    first_grad = jnp.concatenate(
        [
            grad_qkv[:, : 3 * out_cols].reshape(groups, twins * rows, -1),
            out_back.reshape(groups, twins * rows, out_cols),
        ],
        axis=2,
    )
    marks = []
    first_sum = group.scatter(first_grad, 1, marks)
    hidden = jnp.dot(normed_mlp, in_all, preferred_element_type=wide) + bias_in_own
    share_below = 0.5 + 0.5 * lax.erf(hidden * 0.5**0.5)
    act_half = (hidden * share_below).astype(half)
    grad_down = lax.dot_general(
        act_half, cot_flat, (((0,), (0,)), ((), ())), preferred_element_type=wide
    ).astype(half)
    sent = []
    back_cot = after(cot_flat, grad_down, *marks)
    grad_act = contract(back_cot, down_all, 1, 1)
    density = jnp.exp(-0.5 * hidden * hidden) * (2.0 * np.pi) ** -0.5
    grad_hidden = grad_act * (share_below + hidden * density)
    hidden_half = grad_hidden.astype(half)
    grad_in = lax.dot_general(
        normed_mlp, hidden_half, (((0,), (0,)), ((), ())), preferred_element_type=wide
    ).astype(half)
    partial_mlp = lax.dot_general(
        hidden_half, in_all, (((1,), (1,)), ((), ())), preferred_element_type=wide
    )
    partial_out = contract(mixed, out_all, 1, 0) + contract(act_half, down_all, 1, 0)
    branch = group.reduce_sequences(partial_out.reshape(seqs, length, D), sent)
    output = (tokens.astype(wide) + branch + (bias_out + bias_down)).astype(half)

    partial_slope = partial_attn * gain_one + partial_mlp * gain_two
    own = batch * length
    own_unit = unit[:own]
    own_cot = cotangent.reshape(own, D).astype(wide)
    slope = group.reduce_sequences(partial_slope.reshape(seqs, length, D), sent)
    slope = slope.reshape(own, D)
    down_marks = []
    down_total = group.from_replicas(
        group.scatter(grad_down.reshape(groups, units, D), 1, down_marks).astype(half)
    )
    scale = lax.rsqrt(spread[:own] + norm_eps)
    back = scale * (
        slope
        - jnp.mean(slope, axis=-1, keepdims=True)
        - own_unit * jnp.mean(slope * own_unit, axis=-1, keepdims=True)
    )
    input_grad = (own_cot + back).reshape(batch, length, D)

    def columns(values, outer):
        zero = jnp.zeros((outer, ways, values.shape[0] // outer), wide)
        return lax.dynamic_update_slice(
            zero, values.reshape(outer, 1, -1), (0, group.rank, 0)
        ).reshape(-1)

    column_sum = jnp.sum(own_cot, axis=0)
    vector_grad = jnp.concatenate(
        [
            jnp.sum(partial_attn * unit, axis=0),
            jnp.sum(partial_attn, axis=0),
            jnp.sum(partial_mlp * unit, axis=0),
            jnp.sum(partial_mlp, axis=0),
            columns(bias_qkv_grad, 3),
            column_sum,
            columns(jnp.sum(grad_hidden, axis=0), groups),
            column_sum,
        ]
    ).reshape(groups, twins, vec_size)
    vector_grad = jnp.pad(
        vector_grad.astype(half), ((0, 0), (0, 0), (0, vec_rows * width - vec_size))
    ).reshape(groups, twins, vec_rows, width)
    in_grad = jnp.concatenate([grad_in.reshape(groups, twins, rows, width), vector_grad], axis=2)
    in_marks = []
    in_total = group.unshare(group.scatter(in_grad, 2, in_marks, sent))
    first_sum = after(first_sum, *in_marks)
    first_total = group.unshare(first_sum[:, : 3 * out_cols].reshape(twins, rows, -1))
    out_sum = first_sum[:, 3 * out_cols :].astype(half).reshape(ways, out_rows, out_cols)
    out_sum = out_sum.transpose(1, 0, 2).reshape(out_rows, D)
    out_total = group.from_replicas(group.to_holders(out_sum)).reshape(rows, D)
    vec_total = jnp.sum(in_total[:, rows:].astype(wide), axis=0).reshape(-1)[:vec_size]

    totals = (
        first_total.reshape(ways, rows, 3, out_cols)
        .transpose(1, 2, 0, 3)
        .reshape(rows, -1)
        .astype(wide),
        out_total.astype(wide),
        in_total[:, :rows]
        .reshape(ways, rows, groups, units)
        .transpose(1, 2, 0, 3)
        .reshape(rows, -1)
        .astype(wide),
        down_total.reshape(-1, D).astype(wide),
        vec_total,
    )
    masters = (w_qkv, w_out, w_in, w_down, vectors)
    firsts = (m_qkv, m_out, m_in, m_down, m_vec)
    seconds = (v_qkv, v_out, v_in, v_down, v_vec)
    decays = (decay_rate, decay_rate, decay_rate, decay_rate, 0.0)
    results = [
        adamw(masters[number], totals[number], firsts[number], seconds[number], decays[number])
        for number in range(5)
    ]
    return (
        output,
        input_grad,
        *totals,
        *(result[0] for result in results),
        *(result[1] for result in results),
        *(result[2] for result in results),
    )


def solution(mesh):
    placed = (
        P(("shard", "replica"), None, None),
        P(("shard", "replica"), None),
        P(("shard", "replica"), None, None),
        P("shard", None),
        P("shard", None),
        P("shard", None),
        P("shard", None),
        P("shard"),
        P("shard", None),
        P("shard", None),
        P("shard", None),
        P("shard", None),
        P("shard"),
        P("shard", None),
        P("shard", None),
        P("shard", None),
        P("shard", None),
        P("shard"),
    )
    return jax.shard_map(
        functools.partial(step, Group(mesh)),
        mesh=mesh,
        in_specs=placed,
        out_specs=(
            P(("shard", "replica"), None, None),
            P(("shard", "replica"), None, None),
            P("shard", None),
            P("shard", None),
            P("shard", None),
            P("shard", None),
            P("shard"),
            P("shard", None),
            P("shard", None),
            P("shard", None),
            P("shard", None),
            P("shard"),
            P("shard", None),
            P("shard", None),
            P("shard", None),
            P("shard", None),
            P("shard"),
            P("shard", None),
            P("shard", None),
            P("shard", None),
            P("shard", None),
            P("shard"),
        ),
        check_vma=False,
    )
```
